256 devices in a mesh: ctx: 32 (over y, z), heads: 8 (over x, core).
Axes of the slice: x: 4, y: 4, z: 8, core: 2. Of those that a mesh axis runs over, the one named last changes fastest.
Arguments:
- queries: bfloat16 [32768, 4096], P('ctx', 'heads'), may hold values from -8 to 8
- keys: bfloat16 [32768, 4096], P('ctx', 'heads'), may hold values from -8 to 8
- values: bfloat16 [32768, 4096], P('ctx', 'heads'), may hold values from -8 to 8
- gate_bias: float32 [32], P('heads'), may hold values from -2 to 2
- out_weight: bfloat16 [4096, 4096], P('heads'), may hold values from -0.09375 to 0.09375
Outputs:
- layer_out: bfloat16 [32768, 4096], P('ctx', 'heads')
The draws below stay inside these ranges and needn't reach their ends.
All inputs are finite; a program needn't handle non-finite values.
Results may differ from the reference program's by a relative error of at most 0.0051.
Values may be sent and summed in bfloat16 or wider, within the bound.
No kernel may reach another device: no remote copies, remote signals or barrier semaphores. Data moves between devices by JAX's collectives and lax.ppermute only.
A program may use at most 128 MiB of HBM per device.

```python
import math
import jax
import jax.numpy as jnp
from jax import lax

D = 4096
HEADS = 32
HD = 128
SEG = 1024
TOKENS = 32768


class_count = 4


class_strength = 2.0


value_center = 1.6


def query_key_pair(key):
    folded = jax.random.fold_in(key, 11)
    seed_query = jax.random.fold_in(folded, 0)
    seed_key = jax.random.fold_in(folded, 1)
    seed_dirs = jax.random.fold_in(folded, 3)
    seed_qclass = jax.random.fold_in(folded, 4)
    seed_kclass = jax.random.fold_in(folded, 5)
    shape_full = (TOKENS, HEADS * HD)
    class_dirs = jax.random.rademacher(seed_dirs, (class_count, HEADS * HD)).astype(jnp.float32)
    query_class = jax.random.randint(seed_qclass, (TOKENS, HEADS), 0, class_count)
    key_class = jax.random.randint(seed_kclass, (TOKENS, HEADS), 0, class_count)
    query_dir = jnp.take_along_axis(class_dirs, jnp.repeat(query_class, HD, axis=1), axis=0)
    key_dir = jnp.take_along_axis(class_dirs, jnp.repeat(key_class, HD, axis=1), axis=0)
    query_noise = jnp.clip(jax.random.normal(seed_query, shape_full, jnp.float32), -4.0, 4.0)
    key_noise = jnp.clip(jax.random.normal(seed_key, shape_full, jnp.float32), -4.0, 4.0)
    query_draw = class_strength * query_dir + query_noise
    key_draw = class_strength * key_dir + key_noise
    return (jnp.clip(query_draw, -8.0, 8.0), jnp.clip(key_draw, -8.0, 8.0))


def draw_queries(key, part):
    return query_key_pair(key)[0].astype(jnp.bfloat16)


def draw_keys(key, part):
    return query_key_pair(key)[1].astype(jnp.bfloat16)


def draw_values(key, part):
    key_draw = query_key_pair(key)[1]
    folded = jax.random.fold_in(key, 23)
    seed_base, seed_offset, seed_mixing = jax.random.split(folded, 3)
    shape_full = (TOKENS, HEADS * HD)
    mixing = jax.random.normal(seed_mixing, (HEADS, HD, HD), jnp.float32) / math.sqrt(HD)
    centered = (jax.nn.elu(key_draw) + 1.0 - value_center).reshape(TOKENS, HEADS, HD)
    linked = jnp.einsum('thd,hde->the', centered, mixing, precision=lax.Precision.HIGHEST).reshape(shape_full)
    base_draw = jnp.clip(jax.random.normal(seed_base, shape_full, jnp.float32), -4.0, 4.0)
    offsets = jnp.clip(jax.random.normal(seed_offset, (TOKENS // SEG, HEADS * HD), jnp.float32), -3.0, 3.0)
    total = linked + 0.5 * base_draw + jnp.repeat(offsets, SEG, axis=0)
    return jnp.clip(total, -8.0, 8.0).astype(jnp.bfloat16)


def shard_levels(stream_key, extent, cuts, smallest, high):
    def one(dim, blocks):
        steps = jax.random.uniform(jax.random.fold_in(jax.random.fold_in(stream_key, 6), dim), (blocks,), jnp.float32, smallest / len(cuts), high / len(cuts))
        return jnp.repeat(jnp.exp(steps), extent[dim] // blocks).reshape((-1,) + (1,) * (len(extent) - dim - 1))

    loudness = one(*cuts[0])
    for cut in cuts[1:]:
        loudness = loudness * one(*cut)
    return loudness


def normal_values(own_key, extent, width, limit, cuts=(), kind=jnp.bfloat16):
    values = width * jax.random.normal(own_key, extent, jnp.float32)
    if cuts:
        values = values * shard_levels(own_key, extent, cuts, -0.22, 0.18)
    return jnp.clip(values, -limit, limit).astype(kind)


def setup_inputs(seed: int = 0) -> dict:
    splits = jax.random.split(jax.random.key(seed), 6)
    return {
        "queries": draw_queries(jax.random.fold_in(splits[5], 71), 0),
        "keys": draw_keys(jax.random.fold_in(splits[5], 71), 0),
        "values": draw_values(jax.random.fold_in(splits[5], 71), 0),
        "gate_bias": jnp.clip(jax.random.uniform(splits[3], (HEADS,), jnp.float32, -2.0, 2.0) * shard_levels(splits[3], (HEADS,), ((0, 8),), -0.4, 0.0), -2.0, 2.0),
        "out_weight": normal_values(splits[4], (HEADS * HD, D), (HEADS * HD) ** -0.5, 0.09375, ((0, 8),)),
    }


masked_score = -1e+30

def features(inputs):
    return jax.nn.elu(inputs) + 1.0

def head_attention(head_inputs):
    query_head, key_head, value_head = head_inputs
    seg_rows = query_head.shape[0]
    highest = lax.Precision.HIGHEST
    scores = jnp.dot(query_head, key_head.T, precision=highest) * (1.0 / math.sqrt(HD))
    positions = lax.iota(jnp.int32, seg_rows)
    allowed = positions[None, :] <= positions[:, None]
    scores = jnp.where(allowed, scores, masked_score)
    row_max = lax.optimization_barrier(jnp.max(scores, axis=-1, keepdims=True))
    weights = jnp.exp(scores - row_max)
    probabilities = (weights / lax.optimization_barrier(jnp.sum(weights, axis=-1, keepdims=True))).astype(jnp.bfloat16)
    return jnp.dot(probabilities.astype(query_head.dtype), value_head, precision=highest)

def local_attention(query_heads, key_heads, value_heads):
    per_head = lax.map(head_attention, (jnp.transpose(query_heads, (1, 0, 2)), jnp.transpose(key_heads, (1, 0, 2)), jnp.transpose(value_heads, (1, 0, 2))))
    return jnp.transpose(per_head, (1, 0, 2))

def reference(queries, keys, values, gate_bias, out_weight):
    segments = TOKENS // SEG
    query_blocks = queries.reshape(segments, SEG, HEADS, HD)
    key_blocks = keys.reshape(segments, SEG, HEADS, HD)
    value_blocks = values.reshape(segments, SEG, HEADS, HD)
    mix_gate = jax.nn.sigmoid(gate_bias.astype(jnp.float32))[None, :, None]
    highest = lax.Precision.HIGHEST

    def segment_step(state, inputs):
        memory, normalizer = state
        query_seg, key_seg, value_seg = inputs
        query_f = query_seg.astype(jnp.float32)
        key_f = key_seg.astype(jnp.float32)
        value_f = value_seg.astype(jnp.float32)
        feat_query = features(query_f)
        feat_key = features(key_f)
        local_out = local_attention(query_f, key_f, value_f)
        numer = jnp.einsum('thd,hde->the', feat_query, memory, precision=highest)
        denom = jnp.maximum(jnp.einsum('thd,hd->th', feat_query, normalizer, precision=highest), 1.0)
        retrieved = numer / denom[..., None]
        attended = (mix_gate * retrieved + (1.0 - mix_gate) * local_out).astype(jnp.bfloat16)
        memory = memory + jnp.einsum('thd,the->hde', feat_key, value_f, precision=highest)
        normalizer = normalizer + lax.optimization_barrier(jnp.sum(feat_key, axis=0))
        return ((memory, normalizer), attended)
    start_state = (jnp.zeros((HEADS, HD, HD), jnp.float32), jnp.zeros((HEADS, HD), jnp.float32))
    final_state, attended = lax.scan(segment_step, start_state, (query_blocks, key_blocks, value_blocks))
    attended = attended.reshape(TOKENS, HEADS * HD)
    return jnp.dot(attended, out_weight, preferred_element_type=jnp.float32).astype(jnp.bfloat16)
```

```python
import functools
import math

import jax
import jax.numpy as jnp
from jax import lax
from jax.experimental import pallas as pl
from jax.experimental.pallas import tpu as pltpu
from jax.sharding import Mesh
from jax.sharding import PartitionSpec as P

HD = 128
PACK = 144
QB = 256
NT = (((1,), (1,)), ((), ()))
TN = (((0,), (0,)), ((), ()))
F32 = jnp.float32
BF16 = jnp.bfloat16


def features(v):
    return jnp.where(v > 0, v + 1.0, jnp.exp(jnp.minimum(v, 0.0)))


def delta_kernel(k_ref, v_ref, o_ref):
    feat = features(k_ref[...].astype(F32))
    o_ref[0, :HD, :] = lax.dot_general(
        v_ref[...], feat.astype(BF16), TN, preferred_element_type=F32
    )
    total = jnp.sum(feat, axis=0, keepdims=True)
    o_ref[0, HD:, :] = jnp.broadcast_to(total, (PACK - HD, HD))


def delta(keys, values):
    rows, cols = keys.shape
    heads = cols // HD
    spec = pl.BlockSpec((rows, HD), lambda h: (0, h))
    return pl.pallas_call(
        delta_kernel,
        grid=(heads,),
        in_specs=[spec, spec],
        out_specs=pl.BlockSpec((1, PACK, HD), lambda h: (h, 0, 0)),
        out_shape=jax.ShapeDtypeStruct((heads, PACK, HD), F32),
        name="delta",
    )(keys, values)


def attention_kernel(q_ref, k_ref, v_ref, o_ref):
    rows = q_ref.shape[0]
    c = math.log2(math.e) / math.sqrt(HD)
    causal = lax.broadcasted_iota(jnp.int32, (QB, QB), 1) <= lax.broadcasted_iota(
        jnp.int32, (QB, QB), 0
    )
    for i in range(rows // QB):
        lo, hi = i * QB, (i + 1) * QB
        q = q_ref[lo:hi, :]
        diag = lax.dot_general(q, k_ref[lo:hi, :], NT, preferred_element_type=F32)
        diag = jnp.where(causal, diag, -1e30)
        top = jnp.max(diag, axis=-1, keepdims=True)
        if lo:
            off = lax.dot_general(q, k_ref[:lo, :], NT, preferred_element_type=F32)
            top = jnp.maximum(top, jnp.max(off, axis=-1, keepdims=True))
        w = jnp.exp2((diag - top) * c)
        norm = jnp.sum(w, axis=-1, keepdims=True)
        out = jnp.dot(w.astype(BF16), v_ref[lo:hi, :], preferred_element_type=F32)
        if lo:
            w = jnp.exp2((off - top) * c)
            norm += jnp.sum(w, axis=-1, keepdims=True)
            out += jnp.dot(w.astype(BF16), v_ref[:lo, :], preferred_element_type=F32)
        o_ref[lo:hi, :] = out / norm


def attention(queries, keys, values, first, count):
    rows = queries.shape[0]
    spec = pl.BlockSpec((rows, HD), lambda h: (0, first + h))
    return pl.pallas_call(
        attention_kernel,
        grid=(count,),
        in_specs=[spec] * 3,
        out_specs=pl.BlockSpec((rows, HD), lambda h: (0, h)),
        out_shape=jax.ShapeDtypeStruct((rows, count * HD), F32),
        name="attention",
    )(queries, keys, values)


def retrieve_kernel(q_ref, la_ref, lb_ref, s_ref, g_ref, o_ref):
    heads = s_ref.shape[0]
    half = heads // 2
    for h in range(heads):
        cols = slice(h * HD, (h + 1) * HD)
        feat = features(q_ref[:, cols].astype(F32)).astype(BF16)
        got = lax.dot_general(feat, s_ref[h], NT, preferred_element_type=F32)
        denom = jnp.maximum(got[:, HD : HD + 1], 1.0)
        gate = g_ref[:, cols]
        src = la_ref if h < half else lb_ref
        at = h % half
        local = src[:, at * HD : (at + 1) * HD]
        mixed = gate * (got[:, :HD] / denom) + (1.0 - gate) * local
        o_ref[:, cols] = mixed.astype(BF16)


def retrieve(queries, local_a, local_b, state, gate):
    rows, cols = queries.shape
    heads = cols // HD
    block = 256
    return pl.pallas_call(
        retrieve_kernel,
        grid=(rows // block,),
        in_specs=[
            pl.BlockSpec((block, cols), lambda i: (i, 0)),
            pl.BlockSpec((block, cols // 2), lambda i: (i, 0)),
            pl.BlockSpec((block, cols // 2), lambda i: (i, 0)),
            pl.BlockSpec((heads, PACK, HD), lambda i: (0, 0, 0)),
            pl.BlockSpec((1, cols), lambda i: (0, 0)),
        ],
        out_specs=pl.BlockSpec((block, cols), lambda i: (i, 0)),
        out_shape=jax.ShapeDtypeStruct((rows, cols), BF16),
        name="retrieve",
    )(queries, local_a, local_b, state, gate)


def project_kernel(n_add, *refs):
    (ao1, as1, wo1, ws1, ao2, as2, wo2, ws2) = refs[:8]
    adds = refs[8 : 8 + 2 * n_add]
    outs = refs[8 + 2 * n_add :]
    for side, (ao, asb, wo, ws) in enumerate(((ao1, as1, wo1, ws1), (ao2, as2, wo2, ws2))):
        total = jnp.dot(ao[...], wo[0], preferred_element_type=F32)
        total += jnp.dot(asb[...], ws[0], preferred_element_type=F32)
        for j in range(n_add):
            total += adds[2 * j + side][...].astype(F32)
        outs[side][...] = total.astype(outs[side].dtype)


def project(a_own, a_sib, w_own, w_sib, pick, adds, dtype):
    rows, depth = a_own.shape
    width = w_own.shape[2]
    block = 256
    steps = rows // 2 // block
    half = pl.BlockSpec((block, width), lambda i: (i, 0))
    specs, args = [], []
    for side in range(2):
        a_spec = pl.BlockSpec((block, depth), functools.partial(lambda s, i: (s * steps + i, 0), side))
        w_spec = pl.BlockSpec((1, depth, width), functools.partial(lambda k, i: (k, 0, 0), pick[side]))
        specs += [a_spec, a_spec, w_spec, w_spec]
        args += [a_own, a_sib, w_own, w_sib]
    for pair in adds:
        specs += [half, half]
        args += list(pair)
    return pl.pallas_call(
        functools.partial(project_kernel, len(adds)),
        grid=(steps,),
        in_specs=specs,
        out_specs=[half, half],
        out_shape=[jax.ShapeDtypeStruct((rows // 2, width), dtype)] * 2,
        name="project",
    )(*args)


def finish_kernel(steps, p1, p2, r1, r2, o_ref):
    first = pl.program_id(0) < steps

    @pl.when(first)
    def _():
        o_ref[...] = (p1[...] + r1[...].astype(F32)).astype(o_ref.dtype)

    @pl.when(jnp.logical_not(first))
    def _():
        o_ref[...] = (p2[...] + r2[...].astype(F32)).astype(o_ref.dtype)


def finish(p1, p2, r1, r2):
    rows, width = p1.shape
    block = 256
    steps = rows // block
    one = pl.BlockSpec((block, width), lambda i: (jnp.minimum(i, steps - 1), 0))
    two = pl.BlockSpec((block, width), lambda i: (jnp.maximum(i - steps, 0), 0))
    return pl.pallas_call(
        functools.partial(finish_kernel, steps),
        grid=(2 * steps,),
        in_specs=[one, two, one, two],
        out_specs=pl.BlockSpec((block, width), lambda i: (i, 0)),
        out_shape=jax.ShapeDtypeStruct((2 * rows, width), BF16),
        name="finish",
    )(p1, p2, r1, r2)


def swap(array, axis, mask):
    size = lax.axis_size(axis)
    return lax.ppermute(array, axis, [(i, i ^ mask) for i in range(size)])


def entering(own):
    y, z = lax.axis_index("y"), lax.axis_index("z")
    total, before = own, jnp.zeros_like(own)
    for axis, mine, masks in (("z", z, (1, 2, 3)), ("z", z, (4,)), ("y", y, (1, 2, 3))):
        sent = total.astype(BF16)
        got = [swap(sent, axis, m).astype(F32) for m in masks]
        for m, g in zip(masks, got):
            before = before + jnp.where((mine ^ m) < mine, g, 0.0)
            total = total + g
    return before.astype(BF16)


def local(queries, keys, values, gate_bias, out_weight):
    x, c = lax.axis_index("x"), lax.axis_index("c")
    width = out_weight.shape[1] // 8
    own = delta(keys, values)
    state = entering(own)

    def columns(core):
        return jnp.stack(
            [
                lax.dynamic_slice_in_dim(out_weight, ((x ^ k) * 2 + core) * width, width, 1)
                for k in range(4)
            ]
        )

    w_own = columns(c)
    w_sib = swap(columns(1 - c), "c", 1)
    heads = gate_bias.shape[0]
    local_a = attention(queries, keys, values, 0, heads // 2)
    local_b = attention(queries, keys, values, heads // 2, heads // 2)
    gate = jnp.repeat(jax.nn.sigmoid(gate_bias), HD)[None, :]
    a_own = retrieve(queries, local_a, local_b, state, gate)
    a_sib = swap(a_own, "c", 1)

    mm = functools.partial(project, a_own, a_sib, w_own, w_sib)
    far1, far2 = mm((2, 2), (), BF16)
    far1, far2 = swap(far1, "x", 1), swap(far2, "x", 3)
    near1, near2 = mm((1, 3), (), BF16)
    near1, near2 = swap(near1, "x", 1), swap(near2, "x", 3)
    pass1, pass2 = mm((3, 1), ((far1, far2),), BF16)
    pass1, pass2 = swap(pass1, "x", 3), swap(pass2, "x", 1)
    mine1, mine2 = mm((0, 0), ((near1, near2),), F32)
    return finish(mine1, mine2, pass1, pass2)


def solution(mesh):
    finer = Mesh(mesh.devices.reshape(4, 8, 4, 2), ("y", "z", "x", "c"))
    rows, cols = ("y", "z"), ("x", "c")
    placed = (P(rows, cols), P(rows, cols), P(rows, cols), P(cols), P(cols, None))
    return jax.shard_map(
        local, mesh=finer, in_specs=placed, out_specs=P(rows, cols), check_vma=False
    )
```

```python
import functools
import math

import jax
import jax.numpy as jnp
from jax import lax
from jax.experimental import pallas as pl
from jax.experimental.pallas import tpu as pltpu
from jax.sharding import Mesh
from jax.sharding import PartitionSpec as P

HD = 128
PAD = 16
QB = 256
NT = (((1,), (1,)), ((), ()))
TN = (((0,), (0,)), ((), ()))
F32 = jnp.float32
BF16 = jnp.bfloat16
VMEM = pl.BlockSpec(memory_space=pltpu.VMEM)
SMEM = pl.BlockSpec(memory_space=pltpu.SMEM)
PARAMS = pltpu.CompilerParams(vmem_limit_bytes=8 * 2**20)


def near_core(array):
    return pltpu.with_memory_space_constraint(array, pltpu.VMEM)


def far_memory(array):
    return pltpu.with_memory_space_constraint(array, pltpu.HBM)


def features(v):
    return jnp.where(v > 0, v + 1.0, jnp.exp(jnp.minimum(v, 0.0)))


def delta_kernel(k_ref, v_ref, o_ref, total_ref, norm_ref):
    step = pl.program_id(0)
    heads = total_ref.shape[0] // HD

    @pl.when(step == 0)
    def _():
        total_ref[...] = jnp.zeros_like(total_ref)
        norm_ref[...] = jnp.zeros_like(norm_ref)

    feat = features(k_ref[...].astype(F32))
    norm_ref[...] += jnp.sum(feat, axis=0, keepdims=True)
    feat = feat.astype(BF16)
    for h in range(heads):
        cols = slice(h * HD, (h + 1) * HD)
        total_ref[cols, :] += lax.dot_general(
            v_ref[:, cols], feat[:, cols], TN, preferred_element_type=F32
        )

    @pl.when(step == pl.num_programs(0) - 1)
    def _():
        o_ref[: heads * HD, :] = total_ref[...].astype(BF16)
        row = lax.broadcasted_iota(jnp.int32, (PAD, HD), 0)
        norms = jnp.zeros((PAD, HD), F32)
        for h in range(heads):
            mine = jnp.broadcast_to(norm_ref[:, h * HD : (h + 1) * HD], (PAD, HD))
            norms = jnp.where(row == h, mine, norms)
        o_ref[heads * HD :, :] = norms.astype(BF16)


def delta(keys, values):
    rows, cols = keys.shape
    block = 256
    spec = pl.BlockSpec((block, cols), lambda i: (i, 0))
    return pl.pallas_call(
        delta_kernel,
        grid=(rows // block,),
        in_specs=[spec, spec],
        out_specs=VMEM,
        out_shape=pltpu.VMEM((cols + PAD, HD), BF16),
        scratch_shapes=[pltpu.VMEM((cols, HD), F32), pltpu.VMEM((1, cols), F32)],
        compiler_params=PARAMS,
        name="delta",
    )(far_memory(keys), far_memory(values))


def attention_kernel(first, g_ref, q_ref, k_ref, v_ref, o_ref, f_ref):
    h = pl.program_id(0)
    rows = q_ref.shape[0]
    c = math.log2(math.e) / math.sqrt(HD)
    keep = 1.0 - g_ref[first + h]
    causal = lax.broadcasted_iota(jnp.int32, (QB, QB), 1) <= lax.broadcasted_iota(
        jnp.int32, (QB, QB), 0
    )
    for i in range(rows // QB):
        lo, hi = i * QB, (i + 1) * QB
        q = q_ref[lo:hi, :]
        f_ref[lo:hi, :] = features(q.astype(F32)).astype(BF16)
        diag = lax.dot_general(q, k_ref[lo:hi, :], NT, preferred_element_type=F32)
        diag = jnp.where(causal, diag, -1e30)
        top = jnp.max(diag, axis=-1, keepdims=True)
        if lo:
            off = lax.dot_general(q, k_ref[:lo, :], NT, preferred_element_type=F32)
            top = jnp.maximum(top, jnp.max(off, axis=-1, keepdims=True))
        w = jnp.exp2((diag - top) * c)
        norm = jnp.sum(w, axis=-1, keepdims=True)
        out = jnp.dot(w.astype(BF16), v_ref[lo:hi, :], preferred_element_type=F32)
        if lo:
            w = jnp.exp2((off - top) * c)
            norm += jnp.sum(w, axis=-1, keepdims=True)
            out += jnp.dot(w.astype(BF16), v_ref[:lo, :], preferred_element_type=F32)
        o_ref[lo:hi, :] = out * (keep / norm)


def attention(gate, queries, keys, values, first, count):
    rows = queries.shape[0]
    spec = pl.BlockSpec((rows, HD), lambda h: (0, first + h))
    return pl.pallas_call(
        functools.partial(attention_kernel, first),
        grid=(count,),
        in_specs=[SMEM] + [spec] * 3,
        out_specs=[pl.BlockSpec((rows, HD), lambda h: (0, h))] * 2,
        out_shape=[pltpu.HBM((rows, count * HD), F32), pltpu.HBM((rows, count * HD), BF16)],
        compiler_params=PARAMS,
        name="attention",
    )(gate, queries, keys, values)


def retrieve_kernel(g_ref, *refs):
    *groups, s_ref, o_ref = refs
    base = s_ref.shape[0] - PAD
    block = groups[0].shape[0]
    out_rows = pl.ds(pl.multiple_of(pl.program_id(0) * block, block), block)
    h = 0
    for group in range(0, len(groups), 2):
        local, feat = groups[group], groups[group + 1]
        for at in range(local.shape[1] // HD):
            cols = slice(at * HD, (at + 1) * HD)
            f = feat[:, cols]
            numer = lax.dot_general(
                f, s_ref[h * HD : (h + 1) * HD, :], NT, preferred_element_type=F32
            )
            denom = lax.dot_general(f, s_ref[base:, :], NT, preferred_element_type=F32)
            scale = g_ref[h] / jnp.maximum(denom[:, h : h + 1], 1.0)
            mixed = numer * scale + local[:, cols]
            o_ref[out_rows, h * HD : (h + 1) * HD] = mixed.astype(BF16)
            h += 1


def retrieve(gate, groups, state, start, rows):
    flat = [array for group in groups for array in group]
    cols = state.shape[0] - PAD
    block = 128
    first = start // block
    specs = [pl.BlockSpec((block, a.shape[1]), lambda i: (first + i, 0)) for a in flat]
    return pl.pallas_call(
        retrieve_kernel,
        grid=(rows // block,),
        in_specs=[SMEM] + specs + [VMEM],
        out_specs=VMEM,
        out_shape=pltpu.VMEM((rows, cols), BF16),
        compiler_params=PARAMS,
        name="retrieve",
    )(gate, *[far_memory(a) for a in flat], near_core(state))


def sibling_kernel(at_ref, w_ref, o_ref):
    o_ref[0] = w_ref[...]


def sibling_columns(at, weight):
    depth, cols = weight.shape
    width = cols // 8
    return pl.pallas_call(
        sibling_kernel,
        grid_spec=pltpu.PrefetchScalarGridSpec(
            num_scalar_prefetch=1,
            grid=(4,),
            in_specs=[pl.BlockSpec((depth, width), lambda k, at: (0, 2 * k + 1 - at[1]))],
            out_specs=pl.BlockSpec((1, depth, width), lambda k, at: (k, 0, 0)),
        ),
        out_shape=pltpu.HBM((4, depth, width), BF16),
        compiler_params=PARAMS,
        name="sibling_columns",
    )(at, far_memory(weight))


def project_kernel(k, at_ref, a_own, a_sib, w_own, w_sib, *refs):
    *adds, o_ref = refs
    rows, width = o_ref.shape
    to = lax.bitwise_xor(at_ref[0], k)
    cols = pl.ds(pl.multiple_of((to * 2 + at_ref[1]) * width, width), width)
    block = 256
    for lo in range(0, rows, block):
        part = slice(lo, lo + block)
        total = jnp.dot(a_own[part, :], w_own[:, cols], preferred_element_type=F32)
        total += jnp.dot(a_sib[part, :], w_sib[to], preferred_element_type=F32)
        for add in adds:
            total += add[part, :].astype(F32)
        o_ref[part, :] = total.astype(o_ref.dtype)


def project(at, a_own, a_sib, w_own, w_sib, k, adds, dtype):
    rows, width = a_own.shape[0], w_sib.shape[2]
    return pl.pallas_call(
        functools.partial(project_kernel, k),
        in_specs=[SMEM] + [VMEM] * (4 + len(adds)),
        out_specs=VMEM,
        out_shape=pltpu.VMEM((rows, width), dtype),
        compiler_params=PARAMS,
        name="project",
    )(at, *[near_core(a) for a in (a_own, a_sib, w_own, w_sib, *adds)])


def finish_kernel(steps, p1, p2, r1, r2, o_ref):
    i = pl.program_id(0)
    block = o_ref.shape[0]

    def write(p, r, step):
        part = pl.ds(pl.multiple_of(step * block, block), block)
        o_ref[...] = (p[part, :] + r[part, :].astype(F32)).astype(o_ref.dtype)

    @pl.when(i < steps)
    def _():
        write(p1, r1, i)

    @pl.when(i >= steps)
    def _():
        write(p2, r2, i - steps)


def finish(p1, p2, r1, r2):
    rows, width = p1.shape
    block = 256
    steps = rows // block
    return pl.pallas_call(
        functools.partial(finish_kernel, steps),
        grid=(2 * steps,),
        in_specs=[VMEM] * 4,
        out_specs=pl.BlockSpec((block, width), lambda i: (i, 0)),
        out_shape=jax.ShapeDtypeStruct((2 * rows, width), BF16),
        compiler_params=PARAMS,
        name="finish",
    )(*[near_core(a) for a in (p1, p2, r1, r2)])


def swap(array, axis, mask):
    size = lax.axis_size(axis)
    return lax.ppermute(array, axis, [(i, i ^ mask) for i in range(size)])


def local(queries, keys, values, gate_bias, out_weight):
    y, z = lax.axis_index("y"), lax.axis_index("z")
    at = jnp.stack([lax.axis_index("x"), lax.axis_index("c")])
    heads = gate_bias.shape[0]
    gate = jax.nn.sigmoid(gate_bias)
    own = delta(keys, values)
    total, before = own.astype(F32), 0.0
    groups = []

    def fold(axis, mine, masks, beside):
        nonlocal total, before
        got = [swap(total.astype(BF16), axis, m) for m in masks]
        got, beside = lax.optimization_barrier((got, beside))
        for m, g in zip(masks, got):
            g = g.astype(F32)
            before = before + jnp.where((mine ^ m) < mine, g, 0.0)
            total = total + g
        return beside

    first = attention(gate, queries, keys, values, 0, heads // 2)
    first = fold("z", z, (1, 2, 3), first)
    held, total = lax.optimization_barrier(((queries, keys, values), total))
    second = attention(gate, *held, heads // 2, heads // 2)
    second = fold("z", z, (4,), second)
    weight, total = lax.optimization_barrier((out_weight, total))
    w_out = sibling_columns(at, weight)
    w_out = fold("y", y, (1, 2, 3), w_out)
    w_own, w_sib = out_weight, swap(w_out, "c", 1)
    state = before.astype(BF16)

    half = queries.shape[0] // 2
    halves = []
    for start in (0, half):
        a_own = retrieve(gate, (first, second), state, start, half)
        halves.append((a_own, swap(a_own, "c", 1)))

    def mm(i, k, adds, dtype):
        return project(at, *halves[i], w_own, w_sib, k, adds, dtype)

    hops = ((1, 3), (3, 1))
    far = [swap(mm(i, 2, (), BF16), "x", hops[i][0]) for i in range(2)]
    near = [swap(mm(i, hops[i][0], (), BF16), "x", hops[i][0]) for i in range(2)]
    passed = [swap(mm(i, hops[i][1], (far[i],), BF16), "x", hops[i][1]) for i in range(2)]
    mine = [mm(i, 0, (near[i],), F32) for i in range(2)]
    return finish(*mine, *passed)


def solution(mesh):
    finer = Mesh(mesh.devices.reshape(4, 8, 4, 2), ("y", "z", "x", "c"))
    rows, cols = ("y", "z"), ("x", "c")
    placed = (P(rows, cols), P(rows, cols), P(rows, cols), P(cols), P(cols, None))
    return jax.shard_map(
        local, mesh=finer, in_specs=placed, out_specs=P(rows, cols), check_vma=False
    )
```

```python
import functools
import math

import jax
import jax.numpy as jnp
from jax import lax
from jax.experimental import pallas as pl
from jax.experimental.pallas import tpu as pltpu
from jax.sharding import Mesh
from jax.sharding import PartitionSpec as P

HD = 128
PAD = 16
QB = 256
NT = (((1,), (1,)), ((), ()))
TN = (((0,), (0,)), ((), ()))
F32 = jnp.float32
BF16 = jnp.bfloat16
VMEM = pl.BlockSpec(memory_space=pltpu.VMEM)
SMEM = pl.BlockSpec(memory_space=pltpu.SMEM)
PARAMS = pltpu.CompilerParams(vmem_limit_bytes=8 * 2**20)


def near_core(array):
    return pltpu.with_memory_space_constraint(array, pltpu.VMEM)


def far_memory(array):
    return pltpu.with_memory_space_constraint(array, pltpu.HBM)


def features(v):
    return jnp.where(v > 0, v + 1.0, jnp.exp(jnp.minimum(v, 0.0)))


def delta_kernel(k_ref, v_ref, o_ref, total_ref, norm_ref):
    step = pl.program_id(0)
    heads = total_ref.shape[0] // HD

    @pl.when(step == 0)
    def _():
        total_ref[...] = jnp.zeros_like(total_ref)
        norm_ref[...] = jnp.zeros_like(norm_ref)

    feat = features(k_ref[...].astype(F32))
    norm_ref[...] += jnp.sum(feat, axis=0, keepdims=True)
    feat = feat.astype(BF16)
    for h in range(heads):
        cols = slice(h * HD, (h + 1) * HD)
        total_ref[cols, :] += lax.dot_general(
            v_ref[:, cols], feat[:, cols], TN, preferred_element_type=F32
        )

    @pl.when(step == pl.num_programs(0) - 1)
    def _():
        o_ref[: heads * HD, :] = total_ref[...].astype(BF16)
        row = lax.broadcasted_iota(jnp.int32, (PAD, HD), 0)
        norms = jnp.zeros((PAD, HD), F32)
        for h in range(heads):
            mine = jnp.broadcast_to(norm_ref[:, h * HD : (h + 1) * HD], (PAD, HD))
            norms = jnp.where(row == h, mine, norms)
        o_ref[heads * HD :, :] = norms.astype(BF16)


def delta(keys, values):
    rows, cols = keys.shape
    block = 512
    spec = pl.BlockSpec((block, cols), lambda i: (i, 0))
    return pl.pallas_call(
        delta_kernel,
        grid=(rows // block,),
        in_specs=[spec, spec],
        out_specs=VMEM,
        out_shape=pltpu.VMEM((cols + PAD, HD), BF16),
        scratch_shapes=[pltpu.VMEM((cols, HD), F32), pltpu.VMEM((1, cols), F32)],
        compiler_params=PARAMS,
        name="delta",
    )(far_memory(keys), far_memory(values))


def attention_kernel(first, g_ref, q_ref, k_ref, v_ref, o_ref, f_ref):
    h = pl.program_id(0)
    rows = q_ref.shape[0]
    c = math.log2(math.e) / math.sqrt(HD)
    keep = 1.0 - g_ref[first + h]
    causal = lax.broadcasted_iota(jnp.int32, (QB, QB), 1) <= lax.broadcasted_iota(
        jnp.int32, (QB, QB), 0
    )
    for i in range(rows // QB):
        lo, hi = i * QB, (i + 1) * QB
        q = q_ref[lo:hi, :]
        f_ref[0, lo:hi, :] = features(q.astype(F32)).astype(BF16)
        diag = lax.dot_general(q, k_ref[lo:hi, :], NT, preferred_element_type=F32)
        diag = jnp.where(causal, diag, -1e30)
        top = jnp.max(diag, axis=-1, keepdims=True)
        if lo:
            off = lax.dot_general(q, k_ref[:lo, :], NT, preferred_element_type=F32)
            top = jnp.maximum(top, jnp.max(off, axis=-1, keepdims=True))
        w = jnp.exp2((diag - top) * c)
        norm = jnp.sum(w, axis=-1, keepdims=True)
        out = jnp.dot(w.astype(BF16), v_ref[lo:hi, :], preferred_element_type=F32)
        if lo:
            w = jnp.exp2((off - top) * c)
            norm += jnp.sum(w, axis=-1, keepdims=True)
            out += jnp.dot(w.astype(BF16), v_ref[:lo, :], preferred_element_type=F32)
        o_ref[0, lo:hi, :] = out * (keep / norm)


def attention(gate, queries, keys, values, first, count):
    rows = queries.shape[0]
    spec = pl.BlockSpec((rows, HD), lambda h: (0, first + h))
    return pl.pallas_call(
        functools.partial(attention_kernel, first),
        grid=(count,),
        in_specs=[SMEM] + [spec] * 3,
        out_specs=[pl.BlockSpec((1, rows, HD), lambda h: (h, 0, 0))] * 2,
        out_shape=[pltpu.HBM((count, rows, HD), F32), pltpu.HBM((count, rows, HD), BF16)],
        compiler_params=PARAMS,
        name="attention",
    )(gate, far_memory(queries), far_memory(keys), far_memory(values))


def preload_kernel(*refs):
    half = len(refs) // 2
    sems = refs[-1]
    copies = [
        pltpu.make_async_copy(refs[i], refs[half + i], sems.at[i]) for i in range(half)
    ]
    for copy in copies:
        copy.start()
    for copy in copies:
        copy.wait()


def preload(arrays):
    return pl.pallas_call(
        preload_kernel,
        in_specs=[pl.BlockSpec(memory_space=pltpu.HBM)] * len(arrays),
        out_specs=[VMEM] * len(arrays),
        out_shape=[pltpu.VMEM(a.shape, a.dtype) for a in arrays],
        scratch_shapes=[pltpu.SemaphoreType.DMA((len(arrays),))],
        compiler_params=PARAMS,
        name="preload",
    )(*[far_memory(a) for a in arrays])


def retrieve_kernel(starts, g_ref, *refs):
    *groups, s_ref, o_ref = refs
    base = s_ref.shape[0] - PAD
    block = o_ref.shape[0] // len(starts)
    h = 0
    for group in range(0, len(groups), 2):
        local, feat = groups[group], groups[group + 1]
        for at in range(local.shape[0]):
            for i, lo in enumerate(starts):
                f = feat[at, lo : lo + block, :]
                numer = lax.dot_general(
                    f, s_ref[h * HD : (h + 1) * HD, :], NT, preferred_element_type=F32
                )
                denom = lax.dot_general(f, s_ref[base:, :], NT, preferred_element_type=F32)
                scale = g_ref[h] / jnp.maximum(denom[:, h : h + 1], 1.0)
                mixed = numer * scale + local[at, lo : lo + block, :]
                o_ref[i * block : (i + 1) * block, h * HD : (h + 1) * HD] = mixed.astype(BF16)
            h += 1


def retrieve(gate, arrays, state, starts, rows):
    cols = state.shape[0] - PAD
    return pl.pallas_call(
        functools.partial(retrieve_kernel, starts),
        in_specs=[SMEM] + [VMEM] * (len(arrays) + 1),
        out_specs=VMEM,
        out_shape=pltpu.VMEM((rows, cols), BF16),
        compiler_params=PARAMS,
        name="retrieve",
    )(gate, *[near_core(a) for a in arrays], near_core(state))


def sibling_kernel(at_ref, w_ref, o_ref, sems):
    width = o_ref.shape[2]
    copies = []
    for k in range(o_ref.shape[0]):
        cols = pl.ds(pl.multiple_of((2 * k + 1 - at_ref[1]) * width, width), width)
        copies.append(pltpu.make_async_copy(w_ref.at[:, cols], o_ref.at[k], sems.at[k]))
    for copy in copies:
        copy.start()
    for copy in copies:
        copy.wait()


def sibling_columns(at, weight):
    depth, cols = weight.shape
    return pl.pallas_call(
        sibling_kernel,
        in_specs=[SMEM, pl.BlockSpec(memory_space=pltpu.HBM)],
        out_specs=VMEM,
        out_shape=pltpu.VMEM((4, depth, cols // 8), BF16),
        scratch_shapes=[pltpu.SemaphoreType.DMA((4,))],
        compiler_params=PARAMS,
        name="sibling_columns",
    )(at, far_memory(weight))


def block_product(k, at_ref, a_own, a_sib, part, w_own, w_sib, width):
    to = lax.bitwise_xor(at_ref[0], k)
    cols = pl.ds(pl.multiple_of((to * 2 + at_ref[1]) * width, width), width)
    total = jnp.dot(a_own[part, :], w_own[:, cols], preferred_element_type=F32)
    return total + jnp.dot(a_sib[part, :], w_sib[to], preferred_element_type=F32)


def far_kernel(at_ref, a_own, a_sib, w_own, w_sib, *outs):
    block, width = outs[0].shape
    for i, o_ref in enumerate(outs):
        part = slice(i * block, (i + 1) * block)
        total = block_product(2, at_ref, a_own, a_sib, part, w_own, w_sib, width)
        o_ref[...] = total.astype(o_ref.dtype)


def project_far(at, piece, w_own, w_sib):
    rows, width = piece[0].shape[0], w_sib.shape[2]
    return pl.pallas_call(
        far_kernel,
        in_specs=[SMEM] + [VMEM] * 4,
        out_specs=[VMEM, VMEM],
        out_shape=[pltpu.VMEM((rows // 2, width), BF16)] * 2,
        compiler_params=PARAMS,
        name="project_far",
    )(at, *[near_core(a) for a in (*piece, w_own, w_sib)])


def project_kernel(k, side, at_ref, a_own1, a_sib1, a_own2, a_sib2, w_own, w_sib, *refs):
    *adds, o_ref = refs
    width = o_ref.shape[1]
    block = o_ref.shape[0] // 2
    part = slice(side * block, (side + 1) * block)
    for i, (own, sib) in enumerate(((a_own1, a_sib1), (a_own2, a_sib2))):
        out = slice(i * block, (i + 1) * block)
        total = block_product(k, at_ref, own, sib, part, w_own, w_sib, width)
        if len(adds) == 2:
            total += adds[i][...].astype(F32)
        elif adds:
            total += adds[0][out, :].astype(F32)
        o_ref[out, :] = total.astype(o_ref.dtype)


def project(at, pieces, w_own, w_sib, side, k, adds, dtype):
    rows, width = pieces[0][0].shape[0], w_sib.shape[2]
    flat = [array for piece in pieces for array in piece]
    return pl.pallas_call(
        functools.partial(project_kernel, k, side),
        in_specs=[SMEM] + [VMEM] * (6 + len(adds)),
        out_specs=VMEM,
        out_shape=pltpu.VMEM((rows, width), dtype),
        compiler_params=PARAMS,
        name="project",
    )(at, *[near_core(a) for a in (*flat, w_own, w_sib, *adds)])


def finish_kernel(steps, p1, p2, r1, r2, o_ref):
    i = pl.program_id(0)
    block = o_ref.shape[0]

    def write(p, r, step):
        part = pl.ds(pl.multiple_of(step * block, block), block)
        o_ref[...] = (p[part, :] + r[part, :].astype(F32)).astype(o_ref.dtype)

    @pl.when(i < steps)
    def _():
        write(p1, r1, i)

    @pl.when(i >= steps)
    def _():
        write(p2, r2, i - steps)


def finish(p1, p2, r1, r2):
    rows, width = p1.shape
    block = 256
    steps = rows // block
    return pl.pallas_call(
        functools.partial(finish_kernel, steps),
        grid=(2 * steps,),
        in_specs=[VMEM] * 4,
        out_specs=pl.BlockSpec((block, width), lambda i: (i, 0)),
        out_shape=jax.ShapeDtypeStruct((2 * rows, width), BF16),
        compiler_params=PARAMS,
        name="finish",
    )(*[near_core(a) for a in (p1, p2, r1, r2)])


def swap(array, axis, mask):
    size = lax.axis_size(axis)
    return lax.ppermute(array, axis, [(i, i ^ mask) for i in range(size)])


def local(queries, keys, values, gate_bias, out_weight):
    y, z = lax.axis_index("y"), lax.axis_index("z")
    at = jnp.stack([lax.axis_index("x"), lax.axis_index("c")])
    heads = gate_bias.shape[0]
    gate = jax.nn.sigmoid(gate_bias)
    own = delta(keys, values)
    total, before = own.astype(F32), 0.0

    def fold(axis, mine, masks, beside):
        nonlocal total, before
        got = [swap(total.astype(BF16), axis, m) for m in masks]
        got, beside = lax.optimization_barrier((got, beside))
        for m, g in zip(masks, got):
            g = g.astype(F32)
            before = before + jnp.where((mine ^ m) < mine, g, 0.0)
            total = total + g
        total, before = lax.optimization_barrier((total, before))
        return beside

    weight, _ = lax.optimization_barrier((out_weight, own))
    w_out = fold("z", z, (1,), sibling_columns(at, weight))

    w_own, w_sib = out_weight, swap(w_out, "c", 1)

    def heads_after(done, start):
        held, _ = lax.optimization_barrier(((queries, keys, values), done))
        return attention(gate, *held, start, heads // 2)

    first = fold("z", z, (2,), heads_after(total, 0))
    second = fold("z", z, (7,), heads_after(total, heads // 2))
    waiting = (*first, *second)
    waiting, _ = lax.optimization_barrier((waiting, total))
    arrays = fold("y", y, (1, 2, 3), preload(waiting))
    state = before.astype(BF16)

    half = queries.shape[0] // 2
    pieces = []
    for start in (0, half // 2):
        a_own = retrieve(gate, arrays, state, (start, start + half), half)
        pieces.append((a_own, swap(a_own, "c", 1)))

    def mm(side, k, adds, dtype):
        return project(at, pieces, w_own, w_sib, side, k, adds, dtype)

    hops = ((1, 3), (3, 1))
    far = [[], []]
    for piece in pieces:
        for side, part in enumerate(project_far(at, piece, w_own, w_sib)):
            far[side].append(swap(part, "x", hops[side][0]))
    near = [swap(mm(i, hops[i][0], (), BF16), "x", hops[i][0]) for i in range(2)]
    passed = [swap(mm(i, hops[i][1], far[i], BF16), "x", hops[i][1]) for i in range(2)]
    mine = [mm(i, 0, (near[i],), F32) for i in range(2)]
    return finish(*mine, *passed)


def solution(mesh):
    finer = Mesh(mesh.devices.reshape(4, 8, 4, 2), ("y", "z", "x", "c"))
    rows, cols = ("y", "z"), ("x", "c")
    placed = (P(rows, cols), P(rows, cols), P(rows, cols), P(cols), P(cols, None))
    return jax.shard_map(
        local, mesh=finer, in_specs=placed, out_specs=P(rows, cols), check_vma=False
    )
```

```python
import functools
import math

import jax
import jax.numpy as jnp
from jax import lax
from jax.experimental import pallas as pl
from jax.experimental.pallas import tpu as pltpu
from jax.sharding import Mesh
from jax.sharding import PartitionSpec as P

HD = 128
REST = {0: 0, 1: 1, 3: 2}
PAD = 16
QB = 256
NT = (((1,), (1,)), ((), ()))
TN = (((0,), (0,)), ((), ()))
F32 = jnp.float32
BF16 = jnp.bfloat16
VMEM = pl.BlockSpec(memory_space=pltpu.VMEM)
SMEM = pl.BlockSpec(memory_space=pltpu.SMEM)
PARAMS = pltpu.CompilerParams(vmem_limit_bytes=8 * 2**20)


def near_core(array):
    return pltpu.with_memory_space_constraint(array, pltpu.VMEM)


def far_memory(array):
    return pltpu.with_memory_space_constraint(array, pltpu.HBM)


def features(v):
    return jnp.where(v > 0, v + 1.0, jnp.exp(jnp.minimum(v, 0.0)))


def delta_kernel(k_ref, v_ref, o_ref, total_ref, norm_ref):
    step = pl.program_id(0)
    heads = total_ref.shape[0] // HD

    @pl.when(step == 0)
    def _():
        total_ref[...] = jnp.zeros_like(total_ref)
        norm_ref[...] = jnp.zeros_like(norm_ref)

    feat = features(k_ref[...].astype(F32))
    norm_ref[...] += jnp.sum(feat, axis=0, keepdims=True)
    feat = feat.astype(BF16)
    for h in range(heads):
        cols = slice(h * HD, (h + 1) * HD)
        total_ref[cols, :] += lax.dot_general(
            v_ref[:, cols], feat[:, cols], TN, preferred_element_type=F32
        )

    @pl.when(step == pl.num_programs(0) - 1)
    def _():
        o_ref[: heads * HD, :] = total_ref[...].astype(BF16)
        row = lax.broadcasted_iota(jnp.int32, (PAD, HD), 0)
        norms = jnp.zeros((PAD, HD), F32)
        for h in range(heads):
            mine = jnp.broadcast_to(norm_ref[:, h * HD : (h + 1) * HD], (PAD, HD))
            norms = jnp.where(row == h, mine, norms)
        o_ref[heads * HD :, :] = norms.astype(BF16)


def delta(keys, values):
    rows, cols = keys.shape
    block = 512
    spec = pl.BlockSpec((block, cols), lambda i: (i, 0))
    return pl.pallas_call(
        delta_kernel,
        grid=(rows // block,),
        in_specs=[spec, spec],
        out_specs=VMEM,
        out_shape=pltpu.VMEM((cols + PAD, HD), BF16),
        scratch_shapes=[pltpu.VMEM((cols, HD), F32), pltpu.VMEM((1, cols), F32)],
        compiler_params=PARAMS,
        name="delta",
    )(far_memory(keys), far_memory(values))


def attention_kernel(first, g_ref, q_ref, k_ref, v_ref, o_ref, f_ref):
    h = pl.program_id(0)
    rows = q_ref.shape[0]
    c = math.log2(math.e) / math.sqrt(HD)
    keep = 1.0 - g_ref[first + h]
    causal = lax.broadcasted_iota(jnp.int32, (QB, QB), 1) <= lax.broadcasted_iota(
        jnp.int32, (QB, QB), 0
    )
    def scores(i):
        lo, hi = i * QB, (i + 1) * QB
        q = q_ref[lo:hi, :]
        diag = lax.dot_general(q, k_ref[lo:hi, :], NT, preferred_element_type=F32)
        diag = jnp.where(causal, diag, -1e30)
        if not lo:
            return diag, None
        return diag, lax.dot_general(q, k_ref[:lo, :], NT, preferred_element_type=F32)

    blocks = rows // QB
    ahead = scores(0)
    for i in range(blocks):
        lo, hi = i * QB, (i + 1) * QB
        diag, off = ahead
        if i + 1 < blocks:
            ahead = scores(i + 1)
        f_ref[0, lo:hi, :] = features(q_ref[lo:hi, :].astype(F32)).astype(BF16)
        top = jnp.max(diag, axis=-1, keepdims=True)
        if lo:
            top = jnp.maximum(top, jnp.max(off, axis=-1, keepdims=True))
        w = jnp.exp2((diag - top) * c)
        norm = jnp.sum(w, axis=-1, keepdims=True)
        out = jnp.dot(w.astype(BF16), v_ref[lo:hi, :], preferred_element_type=F32)
        if lo:
            w = jnp.exp2((off - top) * c)
            norm += jnp.sum(w, axis=-1, keepdims=True)
            out += jnp.dot(w.astype(BF16), v_ref[:lo, :], preferred_element_type=F32)
        o_ref[0, lo:hi, :] = out * (keep / norm)


def attention(gate, queries, keys, values, first, count):
    rows = queries.shape[0]
    spec = pl.BlockSpec((rows, HD), lambda h: (0, first + h))
    return pl.pallas_call(
        functools.partial(attention_kernel, first),
        grid=(count,),
        in_specs=[SMEM] + [spec] * 3,
        out_specs=[pl.BlockSpec((1, rows, HD), lambda h: (h, 0, 0))] * 2,
        out_shape=[pltpu.HBM((count, rows, HD), F32), pltpu.HBM((count, rows, HD), BF16)],
        compiler_params=PARAMS,
        name="attention",
    )(gate, far_memory(queries), far_memory(keys), far_memory(values))


def preload_kernel(*refs):
    half = len(refs) // 2
    sems = refs[-1]
    copies = [
        pltpu.make_async_copy(refs[i], refs[half + i], sems.at[i]) for i in range(half)
    ]
    for copy in copies:
        copy.start()
    for copy in copies:
        copy.wait()


def preload(arrays):
    return pl.pallas_call(
        preload_kernel,
        in_specs=[pl.BlockSpec(memory_space=pltpu.HBM)] * len(arrays),
        out_specs=[VMEM] * len(arrays),
        out_shape=[pltpu.VMEM(a.shape, a.dtype) for a in arrays],
        scratch_shapes=[pltpu.SemaphoreType.DMA((len(arrays),))],
        compiler_params=PARAMS,
        name="preload",
    )(*[far_memory(a) for a in arrays])


def retrieve_kernel(starts, g_ref, *refs):
    *groups, s_ref, o_ref = refs
    base = s_ref.shape[0] - PAD
    block = o_ref.shape[0] // len(starts)
    h = 0
    for group in range(0, len(groups), 2):
        local, feat = groups[group], groups[group + 1]
        for at in range(local.shape[0]):
            for i, lo in enumerate(starts):
                f = feat[at, lo : lo + block, :]
                numer = lax.dot_general(
                    f, s_ref[h * HD : (h + 1) * HD, :], NT, preferred_element_type=F32
                )
                denom = lax.dot_general(f, s_ref[base:, :], NT, preferred_element_type=F32)
                scale = g_ref[h] / jnp.maximum(denom[:, h : h + 1], 1.0)
                mixed = numer * scale + local[at, lo : lo + block, :]
                o_ref[i * block : (i + 1) * block, h * HD : (h + 1) * HD] = mixed.astype(BF16)
            h += 1


def retrieve(gate, arrays, state, starts, rows):
    cols = state.shape[0] - PAD
    return pl.pallas_call(
        functools.partial(retrieve_kernel, starts),
        in_specs=[SMEM] + [VMEM] * (len(arrays) + 1),
        out_specs=VMEM,
        out_shape=pltpu.VMEM((rows, cols), BF16),
        compiler_params=PARAMS,
        name="retrieve",
    )(gate, *[near_core(a) for a in arrays], near_core(state))


def sibling_kernel(at_ref, w_ref, far_ref, rest_ref, sems):
    width = far_ref.shape[1]
    copies = []
    for k in range(4):
        to = lax.bitwise_xor(at_ref[0], k)
        cols = pl.ds(pl.multiple_of((2 * to + 1 - at_ref[1]) * width, width), width)
        target = far_ref if k == 2 else rest_ref.at[REST[k]]
        copies.append(pltpu.make_async_copy(w_ref.at[:, cols], target, sems.at[k]))
    for copy in copies:
        copy.start()
    for copy in copies:
        copy.wait()


def sibling_columns(at, weight):
    depth, cols = weight.shape
    return pl.pallas_call(
        sibling_kernel,
        in_specs=[SMEM, pl.BlockSpec(memory_space=pltpu.HBM)],
        out_specs=[VMEM, VMEM],
        out_shape=[
            pltpu.VMEM((depth, cols // 8), BF16),
            pltpu.VMEM((3, depth, cols // 8), BF16),
        ],
        scratch_shapes=[pltpu.SemaphoreType.DMA((4,))],
        compiler_params=PARAMS,
        name="sibling_columns",
    )(at, far_memory(weight))


def own_columns(at_ref, k, width):
    to = lax.bitwise_xor(at_ref[0], k)
    return pl.ds(pl.multiple_of((to * 2 + at_ref[1]) * width, width), width)


def far_own_kernel(at_ref, a1, a2, w_own, o1, o2):
    w = w_own[:, own_columns(at_ref, 2, o1.shape[1])]
    for a, o_ref in ((a1, o1), (a2, o2)):
        o_ref[...] = jnp.dot(a[...], w, preferred_element_type=F32)


def far_sibling_kernel(a1, a2, w_sib, p1, p2, o1, o2):
    w = w_sib[...]
    for a, p, o_ref in ((a1, p1, o1), (a2, p2, o2)):
        total = p[...] + jnp.dot(a[...], w, preferred_element_type=F32)
        o_ref[...] = total.astype(o_ref.dtype)


def project_far(at, halves, w_own, w_sib):
    rows, width = halves[0][0].shape[0], w_sib.shape[1]
    (own1, sib1), (own2, sib2) = halves
    partial = pl.pallas_call(
        far_own_kernel,
        in_specs=[SMEM] + [VMEM] * 3,
        out_specs=[VMEM, VMEM],
        out_shape=[pltpu.VMEM((rows, width), F32)] * 2,
        compiler_params=PARAMS,
        name="project_far_own",
    )(at, *[near_core(a) for a in (own1, own2, w_own)])
    return pl.pallas_call(
        far_sibling_kernel,
        in_specs=[VMEM] * 5,
        out_specs=[VMEM, VMEM],
        out_shape=[pltpu.VMEM((rows, width), BF16)] * 2,
        compiler_params=PARAMS,
        name="project_far",
    )(*[near_core(a) for a in (sib1, sib2, w_sib, *partial)])


def project_kernel(k, at_ref, a_own, a_sib, w_own, w_sib, *refs):
    *adds, o_ref = refs
    rows, width = o_ref.shape
    cols = own_columns(at_ref, k, width)
    block = 256
    for lo in range(0, rows, block):
        part = slice(lo, lo + block)
        total = jnp.dot(a_own[part, :], w_own[:, cols], preferred_element_type=F32)
        total += jnp.dot(a_sib[part, :], w_sib[REST[k]], preferred_element_type=F32)
        for add in adds:
            total += add[part, :].astype(F32)
        o_ref[part, :] = total.astype(o_ref.dtype)


def project(at, half, w_own, w_sib, k, adds, dtype):
    rows, width = half[0].shape[0], w_sib.shape[2]
    return pl.pallas_call(
        functools.partial(project_kernel, k),
        in_specs=[SMEM] + [VMEM] * (4 + len(adds)),
        out_specs=VMEM,
        out_shape=pltpu.VMEM((rows, width), dtype),
        compiler_params=PARAMS,
        name="project",
    )(at, *[near_core(a) for a in (*half, w_own, w_sib, *adds)])


def finish_kernel(p_ref, r_ref, *refs):
    o_ref = refs[-1]
    block = o_ref.shape[0]
    part = pl.ds(pl.multiple_of(pl.program_id(0) * block, block), block)
    o_ref[...] = (p_ref[part, :] + r_ref[part, :].astype(F32)).astype(o_ref.dtype)


def finish(total, received, side, before):
    rows, width = total.shape
    block = 256
    steps = rows // block
    rest = [] if before is None else [before]
    return pl.pallas_call(
        finish_kernel,
        grid=(steps,),
        in_specs=[VMEM, VMEM] + [pl.BlockSpec(memory_space=pl.ANY)] * len(rest),
        out_specs=pl.BlockSpec((block, width), lambda i: (side * steps + i, 0)),
        out_shape=jax.ShapeDtypeStruct((2 * rows, width), BF16),
        input_output_aliases={2: 0} if rest else {},
        compiler_params=PARAMS,
        name="finish",
    )(near_core(total), near_core(received), *rest)


def swap(array, axis, mask):
    size = lax.axis_size(axis)
    return lax.ppermute(array, axis, [(i, i ^ mask) for i in range(size)])


def local(queries, keys, values, gate_bias, out_weight):
    y, z = lax.axis_index("y"), lax.axis_index("z")
    at = jnp.stack([lax.axis_index("x"), lax.axis_index("c")])
    heads = gate_bias.shape[0]
    gate = jax.nn.sigmoid(gate_bias)
    own = delta(keys, values)
    total, before = own.astype(F32), 0.0

    def fold(axis, mine, masks, beside):
        nonlocal total, before
        got = [swap(total.astype(BF16), axis, m) for m in masks]
        got, beside = lax.optimization_barrier((got, beside))
        for m, g in zip(masks, got):
            g = g.astype(F32)
            before = before + jnp.where((mine ^ m) < mine, g, 0.0)
            total = total + g
        total, before = lax.optimization_barrier((total, before))
        return beside

    weight, _ = lax.optimization_barrier((out_weight, own))
    w_out = fold("z", z, (1,), sibling_columns(at, weight))

    w_own, w_far = out_weight, swap(w_out[0], "c", 1)

    def heads_after(done):
        held, _ = lax.optimization_barrier(((queries, keys, values), done))
        return attention(gate, *held, 0, heads)

    waiting = fold("z", z, (2, 5, 6), heads_after(total))
    waiting, _ = lax.optimization_barrier((waiting, total))
    arrays, w_far = fold("y", y, (1, 2, 3), (preload(waiting), w_far))
    state = before.astype(BF16)
    w_rest, state = lax.optimization_barrier((w_out[1], state))
    w_sib = swap(w_rest, "c", 1)

    half = queries.shape[0] // 2
    halves = []
    for start in (0, half):
        a_own = retrieve(gate, arrays, state, (start,), half)
        halves.append((a_own, swap(a_own, "c", 1)))

    def mm(side, k, adds, dtype):
        return project(at, halves[side], w_own, w_sib, k, adds, dtype)

    hops = ((1, 3), (3, 1))
    far = project_far(at, halves, w_own, w_far)
    far = [swap(far[i], "x", hops[i][0]) for i in range(2)]
    near = [swap(mm(i, hops[i][0], (), BF16), "x", hops[i][0]) for i in range(2)]
    passed = [swap(mm(i, hops[i][1], (far[i],), BF16), "x", hops[i][1]) for i in range(2)]
    mine = [mm(i, 0, (near[i],), F32) for i in range(2)]
    out = finish(mine[0], passed[0], 0, None)
    return finish(mine[1], passed[1], 1, out)


def solution(mesh):
    finer = Mesh(mesh.devices.reshape(4, 8, 4, 2), ("y", "z", "x", "c"))
    rows, cols = ("y", "z"), ("x", "c")
    placed = (P(rows, cols), P(rows, cols), P(rows, cols), P(cols), P(cols, None))
    return jax.shard_map(
        local, mesh=finer, in_specs=placed, out_specs=P(rows, cols), check_vma=False
    )
```

```python
import functools
import math

import jax
import jax.numpy as jnp
from jax import lax
from jax.experimental import pallas as pl
from jax.experimental.pallas import tpu as pltpu
from jax.sharding import Mesh
from jax.sharding import PartitionSpec as P

HD = 128
REST = {0: 0, 1: 1, 3: 2}
PAD = 16
QB = 256
NT = (((1,), (1,)), ((), ()))
TN = (((0,), (0,)), ((), ()))
F32 = jnp.float32
BF16 = jnp.bfloat16
VMEM = pl.BlockSpec(memory_space=pltpu.VMEM)
SMEM = pl.BlockSpec(memory_space=pltpu.SMEM)
PARAMS = pltpu.CompilerParams(vmem_limit_bytes=8 * 2**20)


def near_core(array):
    return pltpu.with_memory_space_constraint(array, pltpu.VMEM)


def far_memory(array):
    return pltpu.with_memory_space_constraint(array, pltpu.HBM)


def features(v):
    return jnp.where(v > 0, v + 1.0, jnp.exp(jnp.minimum(v, 0.0)))


def delta_kernel(k_ref, v_ref, o_ref, total_ref, norm_ref):
    step = pl.program_id(0)
    heads = total_ref.shape[0] // HD

    @pl.when(step == 0)
    def _():
        total_ref[...] = jnp.zeros_like(total_ref)
        norm_ref[...] = jnp.zeros_like(norm_ref)

    feat = features(k_ref[...].astype(F32))
    norm_ref[...] += jnp.sum(feat, axis=0, keepdims=True)
    feat = feat.astype(BF16)
    for h in range(heads):
        cols = slice(h * HD, (h + 1) * HD)
        total_ref[cols, :] += lax.dot_general(
            v_ref[:, cols], feat[:, cols], TN, preferred_element_type=F32
        )

    @pl.when(step == pl.num_programs(0) - 1)
    def _():
        o_ref[: heads * HD, :] = total_ref[...].astype(BF16)
        row = lax.broadcasted_iota(jnp.int32, (PAD, HD), 0)
        norms = jnp.zeros((PAD, HD), F32)
        for h in range(heads):
            mine = jnp.broadcast_to(norm_ref[:, h * HD : (h + 1) * HD], (PAD, HD))
            norms = jnp.where(row == h, mine, norms)
        o_ref[heads * HD :, :] = norms.astype(BF16)


def delta(keys, values):
    rows, cols = keys.shape
    block = 512
    spec = pl.BlockSpec((block, cols), lambda i: (i, 0))
    return pl.pallas_call(
        delta_kernel,
        grid=(rows // block,),
        in_specs=[spec, spec],
        out_specs=VMEM,
        out_shape=pltpu.VMEM((cols + PAD, HD), BF16),
        scratch_shapes=[pltpu.VMEM((cols, HD), F32), pltpu.VMEM((1, cols), F32)],
        compiler_params=PARAMS,
        name="delta",
    )(far_memory(keys), far_memory(values))


def attention_kernel(first, g_ref, q_ref, k_ref, v_ref, o_ref, f_ref):
    h = pl.program_id(0)
    rows = q_ref.shape[0]
    c = math.log2(math.e) / math.sqrt(HD)
    keep = 1.0 - g_ref[first + h]
    causal = lax.broadcasted_iota(jnp.int32, (QB, QB), 1) <= lax.broadcasted_iota(
        jnp.int32, (QB, QB), 0
    )
    def scores(i):
        lo, hi = i * QB, (i + 1) * QB
        q = q_ref[lo:hi, :]
        diag = lax.dot_general(q, k_ref[lo:hi, :], NT, preferred_element_type=F32)
        diag = jnp.where(causal, diag, -1e30)
        if not lo:
            return diag, None
        return diag, lax.dot_general(q, k_ref[:lo, :], NT, preferred_element_type=F32)

    blocks = rows // QB
    ahead = scores(0)
    for i in range(blocks):
        lo, hi = i * QB, (i + 1) * QB
        diag, off = ahead
        if i + 1 < blocks:
            ahead = scores(i + 1)
        f_ref[0, lo:hi, :] = features(q_ref[lo:hi, :].astype(F32)).astype(BF16)
        top = jnp.max(diag, axis=-1, keepdims=True)
        if lo:
            top = jnp.maximum(top, jnp.max(off, axis=-1, keepdims=True))
        w = jnp.exp2((diag - top) * c)
        norm = jnp.sum(w, axis=-1, keepdims=True)
        out = jnp.dot(w.astype(BF16), v_ref[lo:hi, :], preferred_element_type=F32)
        if lo:
            w = jnp.exp2((off - top) * c)
            norm += jnp.sum(w, axis=-1, keepdims=True)
            out += jnp.dot(w.astype(BF16), v_ref[:lo, :], preferred_element_type=F32)
        o_ref[0, lo:hi, :] = out * (keep / norm)


def attention(gate, queries, keys, values, first, count):
    rows = queries.shape[0]
    spec = pl.BlockSpec((rows, HD), lambda h: (0, first + h))
    return pl.pallas_call(
        functools.partial(attention_kernel, first),
        grid=(count,),
        in_specs=[SMEM] + [spec] * 3,
        out_specs=[pl.BlockSpec((1, rows, HD), lambda h: (h, 0, 0))] * 2,
        out_shape=[pltpu.HBM((count, rows, HD), F32), pltpu.HBM((count, rows, HD), BF16)],
        compiler_params=PARAMS,
        name="attention",
    )(gate, far_memory(queries), far_memory(keys), far_memory(values))


def preload_kernel(*refs):
    half = len(refs) // 2
    sems = refs[-1]
    copies = [
        pltpu.make_async_copy(refs[i], refs[half + i], sems.at[i]) for i in range(half)
    ]
    for copy in copies:
        copy.start()
    for copy in copies:
        copy.wait()


def preload(arrays):
    return pl.pallas_call(
        preload_kernel,
        in_specs=[pl.BlockSpec(memory_space=pltpu.HBM)] * len(arrays),
        out_specs=[VMEM] * len(arrays),
        out_shape=[pltpu.VMEM(a.shape, a.dtype) for a in arrays],
        scratch_shapes=[pltpu.SemaphoreType.DMA((len(arrays),))],
        compiler_params=PARAMS,
        name="preload",
    )(*[far_memory(a) for a in arrays])


def retrieve_kernel(starts, g_ref, *refs):
    *groups, s_ref, o_ref = refs
    base = s_ref.shape[0] - PAD
    block = o_ref.shape[0] // len(starts)
    h = 0
    for group in range(0, len(groups), 2):
        local, feat = groups[group], groups[group + 1]
        for at in range(local.shape[0]):
            for i, lo in enumerate(starts):
                f = feat[at, lo : lo + block, :]
                numer = lax.dot_general(
                    f, s_ref[h * HD : (h + 1) * HD, :], NT, preferred_element_type=F32
                )
                denom = lax.dot_general(f, s_ref[base:, :], NT, preferred_element_type=F32)
                scale = g_ref[h] / jnp.maximum(denom[:, h : h + 1], 1.0)
                mixed = numer * scale + local[at, lo : lo + block, :]
                o_ref[i * block : (i + 1) * block, h * HD : (h + 1) * HD] = mixed.astype(BF16)
            h += 1


def retrieve(gate, arrays, state, starts, rows):
    cols = state.shape[0] - PAD
    return pl.pallas_call(
        functools.partial(retrieve_kernel, starts),
        in_specs=[SMEM] + [VMEM] * (len(arrays) + 1),
        out_specs=VMEM,
        out_shape=pltpu.VMEM((rows, cols), BF16),
        compiler_params=PARAMS,
        name="retrieve",
    )(gate, *[near_core(a) for a in arrays], near_core(state))


def sibling_kernel(at_ref, w_ref, far_ref, rest_ref, sems):
    width = far_ref.shape[1]
    copies = []
    for k in range(4):
        to = lax.bitwise_xor(at_ref[0], k)
        cols = pl.ds(pl.multiple_of((2 * to + 1 - at_ref[1]) * width, width), width)
        target = far_ref if k == 2 else rest_ref.at[REST[k]]
        copies.append(pltpu.make_async_copy(w_ref.at[:, cols], target, sems.at[k]))
    for copy in copies:
        copy.start()
    for copy in copies:
        copy.wait()


def sibling_columns(at, weight):
    depth, cols = weight.shape
    return pl.pallas_call(
        sibling_kernel,
        in_specs=[SMEM, pl.BlockSpec(memory_space=pltpu.HBM)],
        out_specs=[VMEM, VMEM],
        out_shape=[
            pltpu.VMEM((depth, cols // 8), BF16),
            pltpu.VMEM((3, depth, cols // 8), BF16),
        ],
        scratch_shapes=[pltpu.SemaphoreType.DMA((4,))],
        compiler_params=PARAMS,
        name="sibling_columns",
    )(at, far_memory(weight))


def own_columns(at_ref, k, width):
    to = lax.bitwise_xor(at_ref[0], k)
    return pl.ds(pl.multiple_of((to * 2 + at_ref[1]) * width, width), width)


def far_own_kernel(at_ref, a1, a2, w_own, o1, o2):
    w = w_own[:, own_columns(at_ref, 2, o1.shape[1])]
    for a, o_ref in ((a1, o1), (a2, o2)):
        o_ref[...] = jnp.dot(a[...], w, preferred_element_type=F32)


def far_sibling_kernel(a1, a2, w_sib, p1, p2, o1, o2):
    w = w_sib[...]
    for a, p, o_ref in ((a1, p1, o1), (a2, p2, o2)):
        total = p[...] + jnp.dot(a[...], w, preferred_element_type=F32)
        o_ref[...] = total.astype(o_ref.dtype)


def project_far(at, halves, w_own, w_sib):
    rows, width = halves[0][0].shape[0], w_sib.shape[1]
    (own1, sib1), (own2, sib2) = halves
    partial = pl.pallas_call(
        far_own_kernel,
        in_specs=[SMEM] + [VMEM] * 3,
        out_specs=[VMEM, VMEM],
        out_shape=[pltpu.VMEM((rows, width), F32)] * 2,
        compiler_params=PARAMS,
        name="project_far_own",
    )(at, *[near_core(a) for a in (own1, own2, w_own)])
    return pl.pallas_call(
        far_sibling_kernel,
        in_specs=[VMEM] * 5,
        out_specs=[VMEM, VMEM],
        out_shape=[pltpu.VMEM((rows, width), BF16)] * 2,
        compiler_params=PARAMS,
        name="project_far",
    )(*[near_core(a) for a in (sib1, sib2, w_sib, *partial)])


def project_kernel(k, at_ref, a_own, a_sib, w_own, w_sib, *refs):
    *adds, o_ref = refs
    rows, width = o_ref.shape
    cols = own_columns(at_ref, k, width)
    block = 256
    for lo in range(0, rows, block):
        part = slice(lo, lo + block)
        total = jnp.dot(a_own[part, :], w_own[:, cols], preferred_element_type=F32)
        total += jnp.dot(a_sib[part, :], w_sib[REST[k]], preferred_element_type=F32)
        for add in adds:
            total += add[part, :].astype(F32)
        o_ref[part, :] = total.astype(o_ref.dtype)


def project(at, half, w_own, w_sib, k, adds, dtype):
    rows, width = half[0].shape[0], w_sib.shape[2]
    return pl.pallas_call(
        functools.partial(project_kernel, k),
        in_specs=[SMEM] + [VMEM] * (4 + len(adds)),
        out_specs=VMEM,
        out_shape=pltpu.VMEM((rows, width), dtype),
        compiler_params=PARAMS,
        name="project",
    )(at, *[near_core(a) for a in (*half, w_own, w_sib, *adds)])


def finish_kernel(p_ref, r_ref, *refs):
    o_ref = refs[-1]
    block = o_ref.shape[0]
    part = pl.ds(pl.multiple_of(pl.program_id(0) * block, block), block)
    o_ref[...] = (p_ref[part, :] + r_ref[part, :].astype(F32)).astype(o_ref.dtype)


def finish(total, received, side, before):
    rows, width = total.shape
    block = 256
    steps = rows // block
    rest = [] if before is None else [before]
    return pl.pallas_call(
        finish_kernel,
        grid=(steps,),
        in_specs=[VMEM, VMEM] + [pl.BlockSpec(memory_space=pl.ANY)] * len(rest),
        out_specs=pl.BlockSpec((block, width), lambda i: (side * steps + i, 0)),
        out_shape=jax.ShapeDtypeStruct((2 * rows, width), BF16),
        input_output_aliases={2: 0} if rest else {},
        compiler_params=PARAMS,
        name="finish",
    )(near_core(total), near_core(received), *rest)


def swap(array, axis, mask):
    size = lax.axis_size(axis)
    return lax.ppermute(array, axis, [(i, i ^ mask) for i in range(size)])


def local(queries, keys, values, gate_bias, out_weight):
    y, z = lax.axis_index("y"), lax.axis_index("z")
    at = jnp.stack([lax.axis_index("x"), lax.axis_index("c")])
    heads = gate_bias.shape[0]
    gate = jax.nn.sigmoid(gate_bias)
    own = delta(keys, values)
    total, before = own.astype(F32), 0.0

    def fold(axis, mine, masks, beside):
        nonlocal total, before
        got = [swap(total.astype(BF16), axis, m) for m in masks]
        got, beside = lax.optimization_barrier((got, beside))
        for m, g in zip(masks, got):
            g = g.astype(F32)
            before = before + jnp.where((mine ^ m) < mine, g, 0.0)
            total = total + g
        total, before = lax.optimization_barrier((total, before))
        return beside

    weight, _ = lax.optimization_barrier((out_weight, own))
    w_out = fold("z", z, (1,), sibling_columns(at, weight))

    w_own, w_far = out_weight, swap(w_out[0], "c", 1)

    def heads_after(done):
        held, _ = lax.optimization_barrier(((queries, keys, values), done))
        return attention(gate, *held, 0, heads)

    waiting = fold("z", z, (5, 2, 6), heads_after(total))
    waiting, _ = lax.optimization_barrier((waiting, total))
    arrays, w_far = fold("y", y, (2, 1, 3), (preload(waiting), w_far))
    state = before.astype(BF16)
    w_rest, state = lax.optimization_barrier((w_out[1], state))
    w_sib = swap(w_rest, "c", 1)

    half = queries.shape[0] // 2
    halves = []
    for start in (0, half):
        a_own = retrieve(gate, arrays, state, (start,), half)
        halves.append((a_own, swap(a_own, "c", 1)))

    def mm(side, k, adds, dtype):
        return project(at, halves[side], w_own, w_sib, k, adds, dtype)

    hops = ((1, 3), (3, 1))
    far = project_far(at, halves, w_own, w_far)
    far = [swap(far[i], "x", hops[i][0]) for i in range(2)]
    near = [swap(mm(i, hops[i][0], (), BF16), "x", hops[i][0]) for i in range(2)]
    passed = [swap(mm(i, hops[i][1], (far[i],), BF16), "x", hops[i][1]) for i in range(2)]
    mine = [mm(i, 0, (near[i],), F32) for i in range(2)]
    out = finish(mine[0], passed[0], 0, None)
    return finish(mine[1], passed[1], 1, out)


def solution(mesh):
    finer = Mesh(mesh.devices.reshape(4, 8, 4, 2), ("y", "z", "x", "c"))
    rows, cols = ("y", "z"), ("x", "c")
    placed = (P(rows, cols), P(rows, cols), P(rows, cols), P(cols), P(cols, None))
    return jax.shard_map(
        local, mesh=finer, in_specs=placed, out_specs=P(rows, cols), check_vma=False
    )
```

```python
import functools
import math

import jax
import jax.numpy as jnp
from jax import lax
from jax.experimental import pallas as pl
from jax.experimental.pallas import tpu as pltpu
from jax.sharding import Mesh
from jax.sharding import PartitionSpec as P

HD = 128
REST = {0: 0, 1: 1, 3: 2}
PAD = 16
QB = 256
NT = (((1,), (1,)), ((), ()))
TN = (((0,), (0,)), ((), ()))
F32 = jnp.float32
BF16 = jnp.bfloat16
VMEM = pl.BlockSpec(memory_space=pltpu.VMEM)
SMEM = pl.BlockSpec(memory_space=pltpu.SMEM)
PARAMS = pltpu.CompilerParams(vmem_limit_bytes=8 * 2**20)


def near_core(array):
    return pltpu.with_memory_space_constraint(array, pltpu.VMEM)


def far_memory(array):
    return pltpu.with_memory_space_constraint(array, pltpu.HBM)


def features(v):
    return jnp.where(v > 0, v + 1.0, jnp.exp(jnp.minimum(v, 0.0)))


def delta_kernel(k_ref, v_ref, o_ref, total_ref, norm_ref):
    step = pl.program_id(0)
    heads = total_ref.shape[0] // HD

    @pl.when(step == 0)
    def _():
        total_ref[...] = jnp.zeros_like(total_ref)
        norm_ref[...] = jnp.zeros_like(norm_ref)

    feat = features(k_ref[...].astype(F32))
    norm_ref[...] += jnp.sum(feat, axis=0, keepdims=True)
    feat = feat.astype(BF16)
    for h in range(heads):
        cols = slice(h * HD, (h + 1) * HD)
        total_ref[cols, :] += lax.dot_general(
            v_ref[:, cols], feat[:, cols], TN, preferred_element_type=F32
        )

    @pl.when(step == pl.num_programs(0) - 1)
    def _():
        o_ref[: heads * HD, :] = total_ref[...].astype(BF16)
        row = lax.broadcasted_iota(jnp.int32, (PAD, HD), 0)
        norms = jnp.zeros((PAD, HD), F32)
        for h in range(heads):
            mine = jnp.broadcast_to(norm_ref[:, h * HD : (h + 1) * HD], (PAD, HD))
            norms = jnp.where(row == h, mine, norms)
        o_ref[heads * HD :, :] = norms.astype(BF16)


def delta(keys, values):
    rows, cols = keys.shape
    block = 512
    spec = pl.BlockSpec((block, cols), lambda i: (i, 0))
    return pl.pallas_call(
        delta_kernel,
        grid=(rows // block,),
        in_specs=[spec, spec],
        out_specs=VMEM,
        out_shape=pltpu.VMEM((cols + PAD, HD), BF16),
        scratch_shapes=[pltpu.VMEM((cols, HD), F32), pltpu.VMEM((1, cols), F32)],
        compiler_params=PARAMS,
        name="delta",
    )(far_memory(keys), far_memory(values))


def attention_kernel(first, g_ref, q_ref, k_ref, v_ref, o_ref, f_ref):
    h = pl.program_id(0)
    rows = q_ref.shape[0]
    c = math.log2(math.e) / math.sqrt(HD)
    keep = 1.0 - g_ref[first + h]
    causal = lax.broadcasted_iota(jnp.int32, (QB, QB), 1) <= lax.broadcasted_iota(
        jnp.int32, (QB, QB), 0
    )
    def scores(i):
        lo, hi = i * QB, (i + 1) * QB
        q = q_ref[lo:hi, :]
        diag = lax.dot_general(q, k_ref[lo:hi, :], NT, preferred_element_type=F32)
        diag = jnp.where(causal, diag, -1e30)
        if not lo:
            return diag, None
        return diag, lax.dot_general(q, k_ref[:lo, :], NT, preferred_element_type=F32)

    blocks = rows // QB
    ahead = scores(0)
    for i in range(blocks):
        lo, hi = i * QB, (i + 1) * QB
        diag, off = ahead
        if i + 1 < blocks:
            ahead = scores(i + 1)
        f_ref[0, lo:hi, :] = features(q_ref[lo:hi, :].astype(F32)).astype(BF16)
        top = jnp.max(diag, axis=-1, keepdims=True)
        if lo:
            top = jnp.maximum(top, jnp.max(off, axis=-1, keepdims=True))
        w = jnp.exp2((diag - top) * c)
        norm = jnp.sum(w, axis=-1, keepdims=True)
        out = jnp.dot(w.astype(BF16), v_ref[lo:hi, :], preferred_element_type=F32)
        if lo:
            w = jnp.exp2((off - top) * c)
            norm += jnp.sum(w, axis=-1, keepdims=True)
            out += jnp.dot(w.astype(BF16), v_ref[:lo, :], preferred_element_type=F32)
        o_ref[0, lo:hi, :] = out * (keep / norm)


def attention(gate, queries, keys, values, first, count):
    rows = queries.shape[0]
    spec = pl.BlockSpec((rows, HD), lambda h: (0, first + h))
    return pl.pallas_call(
        functools.partial(attention_kernel, first),
        grid=(count,),
        in_specs=[SMEM] + [spec] * 3,
        out_specs=[pl.BlockSpec((1, rows, HD), lambda h: (h, 0, 0))] * 2,
        out_shape=[pltpu.HBM((count, rows, HD), F32), pltpu.HBM((count, rows, HD), BF16)],
        compiler_params=PARAMS,
        name="attention",
    )(gate, far_memory(queries), far_memory(keys), far_memory(values))


def preload_kernel(*refs):
    half = len(refs) // 2
    sems = refs[-1]
    copies = [
        pltpu.make_async_copy(refs[i], refs[half + i], sems.at[i]) for i in range(half)
    ]
    for copy in copies:
        copy.start()
    for copy in copies:
        copy.wait()


def preload(arrays):
    return pl.pallas_call(
        preload_kernel,
        in_specs=[pl.BlockSpec(memory_space=pltpu.HBM)] * len(arrays),
        out_specs=[VMEM] * len(arrays),
        out_shape=[pltpu.VMEM(a.shape, a.dtype) for a in arrays],
        scratch_shapes=[pltpu.SemaphoreType.DMA((len(arrays),))],
        compiler_params=PARAMS,
        name="preload",
    )(*[far_memory(a) for a in arrays])


def retrieve_kernel(g_ref, *refs):
    *groups, s_ref, o1, o2 = refs
    rows = o1.shape[0]
    base = s_ref.shape[0] - PAD
    for side, o_ref in enumerate((o1, o2)):
        h = 0
        part = slice(side * rows, (side + 1) * rows)
        for group in range(0, len(groups), 2):
            local, feat = groups[group], groups[group + 1]
            for at in range(local.shape[0]):
                f = feat[at, part, :]
                numer = lax.dot_general(
                    f, s_ref[h * HD : (h + 1) * HD, :], NT, preferred_element_type=F32
                )
                denom = lax.dot_general(f, s_ref[base:, :], NT, preferred_element_type=F32)
                scale = g_ref[h] / jnp.maximum(denom[:, h : h + 1], 1.0)
                mixed = numer * scale + local[at, part, :]
                o_ref[:, h * HD : (h + 1) * HD] = mixed.astype(BF16)
                h += 1


def retrieve(gate, arrays, state, rows):
    cols = state.shape[0] - PAD
    return pl.pallas_call(
        retrieve_kernel,
        in_specs=[SMEM] + [VMEM] * (len(arrays) + 1),
        out_specs=[VMEM, VMEM],
        out_shape=[pltpu.VMEM((rows // 2, cols), BF16)] * 2,
        compiler_params=PARAMS,
        name="retrieve",
    )(gate, *[near_core(a) for a in arrays], near_core(state))


def sibling_kernel(at_ref, w_ref, far_ref, rest_ref, sems):
    width = far_ref.shape[1]
    copies = []
    for k in range(4):
        to = lax.bitwise_xor(at_ref[0], k)
        cols = pl.ds(pl.multiple_of((2 * to + 1 - at_ref[1]) * width, width), width)
        target = far_ref if k == 2 else rest_ref.at[REST[k]]
        copies.append(pltpu.make_async_copy(w_ref.at[:, cols], target, sems.at[k]))
    for copy in copies:
        copy.start()
    for copy in copies:
        copy.wait()


def sibling_columns(at, weight):
    depth, cols = weight.shape
    return pl.pallas_call(
        sibling_kernel,
        in_specs=[SMEM, pl.BlockSpec(memory_space=pltpu.HBM)],
        out_specs=[VMEM, VMEM],
        out_shape=[
            pltpu.VMEM((depth, cols // 8), BF16),
            pltpu.VMEM((3, depth, cols // 8), BF16),
        ],
        scratch_shapes=[pltpu.SemaphoreType.DMA((4,))],
        compiler_params=PARAMS,
        name="sibling_columns",
    )(at, far_memory(weight))


def own_columns(at_ref, k, width):
    to = lax.bitwise_xor(at_ref[0], k)
    return pl.ds(pl.multiple_of((to * 2 + at_ref[1]) * width, width), width)


def far_own_kernel(at_ref, a1, a2, w_own, o1, o2):
    w = w_own[:, own_columns(at_ref, 2, o1.shape[1])]
    for a, o_ref in ((a1, o1), (a2, o2)):
        o_ref[...] = jnp.dot(a[...], w, preferred_element_type=F32)


def far_sibling_kernel(a1, a2, w_sib, p1, p2, o1, o2):
    w = w_sib[...]
    for a, p, o_ref in ((a1, p1, o1), (a2, p2, o2)):
        total = p[...] + jnp.dot(a[...], w, preferred_element_type=F32)
        o_ref[...] = total.astype(o_ref.dtype)


def project_far(at, halves, w_own, w_sib):
    rows, width = halves[0][0].shape[0], w_sib.shape[1]
    (own1, sib1), (own2, sib2) = halves
    partial = pl.pallas_call(
        far_own_kernel,
        in_specs=[SMEM] + [VMEM] * 3,
        out_specs=[VMEM, VMEM],
        out_shape=[pltpu.VMEM((rows, width), F32)] * 2,
        compiler_params=PARAMS,
        name="project_far_own",
    )(at, *[near_core(a) for a in (own1, own2, w_own)])
    return pl.pallas_call(
        far_sibling_kernel,
        in_specs=[VMEM] * 5,
        out_specs=[VMEM, VMEM],
        out_shape=[pltpu.VMEM((rows, width), BF16)] * 2,
        compiler_params=PARAMS,
        name="project_far",
    )(*[near_core(a) for a in (sib1, sib2, w_sib, *partial)])


def project_kernel(k, at_ref, a_own, a_sib, w_own, w_sib, *refs):
    *adds, o_ref = refs
    rows, width = o_ref.shape
    cols = own_columns(at_ref, k, width)
    block = 256
    for lo in range(0, rows, block):
        part = slice(lo, lo + block)
        total = jnp.dot(a_own[part, :], w_own[:, cols], preferred_element_type=F32)
        total += jnp.dot(a_sib[part, :], w_sib[REST[k]], preferred_element_type=F32)
        for add in adds:
            total += add[part, :].astype(F32)
        o_ref[part, :] = total.astype(o_ref.dtype)


def project(at, half, w_own, w_sib, k, adds, dtype):
    rows, width = half[0].shape[0], w_sib.shape[2]
    return pl.pallas_call(
        functools.partial(project_kernel, k),
        in_specs=[SMEM] + [VMEM] * (4 + len(adds)),
        out_specs=VMEM,
        out_shape=pltpu.VMEM((rows, width), dtype),
        compiler_params=PARAMS,
        name="project",
    )(at, *[near_core(a) for a in (*half, w_own, w_sib, *adds)])


def finish_kernel(p1, p2, r1, r2, o_ref, held, sems):
    rows = p1.shape[0]
    block = held.shape[0] // sems.shape[0]
    copies = []
    for i in range(sems.shape[0]):
        p, r = (p1, r1) if i * block < rows else (p2, r2)
        part = slice(i * block % rows, i * block % rows + block)
        out = slice(i * block, (i + 1) * block)
        held[out, :] = (p[part, :] + r[part, :].astype(F32)).astype(held.dtype)
        copies.append(pltpu.make_async_copy(held.at[out], o_ref.at[out], sems.at[i]))
        copies[-1].start()
    for copy in copies:
        copy.wait()


def finish(p1, p2, r1, r2):
    rows, width = p1.shape
    return pl.pallas_call(
        finish_kernel,
        in_specs=[VMEM] * 4,
        out_specs=pl.BlockSpec(memory_space=pltpu.HBM),
        out_shape=jax.ShapeDtypeStruct((2 * rows, width), BF16),
        scratch_shapes=[pltpu.VMEM((2 * rows, width), BF16), pltpu.SemaphoreType.DMA((4,))],
        compiler_params=PARAMS,
        name="finish",
    )(*[near_core(a) for a in (p1, p2, r1, r2)])


def swap(array, axis, mask):
    size = lax.axis_size(axis)
    return lax.ppermute(array, axis, [(i, i ^ mask) for i in range(size)])


def local(queries, keys, values, gate_bias, out_weight):
    y, z = lax.axis_index("y"), lax.axis_index("z")
    at = jnp.stack([lax.axis_index("x"), lax.axis_index("c")])
    heads = gate_bias.shape[0]
    gate = jax.nn.sigmoid(gate_bias)
    own = delta(keys, values)
    total, before = own.astype(F32), 0.0

    def fold(axis, mine, masks, beside):
        nonlocal total, before
        got = [swap(total.astype(BF16), axis, m) for m in masks]
        got, beside = lax.optimization_barrier((got, beside))
        for m, g in zip(masks, got):
            g = g.astype(F32)
            before = before + jnp.where((mine ^ m) < mine, g, 0.0)
            total = total + g
        total, before = lax.optimization_barrier((total, before))
        return beside

    weight, _ = lax.optimization_barrier((out_weight, own))
    w_out = fold("z", z, (1,), sibling_columns(at, weight))

    w_own, w_far = out_weight, swap(w_out[0], "c", 1)

    def heads_after(done):
        held, _ = lax.optimization_barrier(((queries, keys, values), done))
        return attention(gate, *held, 0, heads)

    waiting = fold("z", z, (5, 6, 2), heads_after(total))
    waiting, _ = lax.optimization_barrier((waiting, total))
    arrays, w_far = fold("y", y, (2, 1, 3), (preload(waiting), w_far))
    state = before.astype(BF16)
    w_rest, state = lax.optimization_barrier((w_out[1], state))
    w_sib = swap(w_rest, "c", 1)

    attended = retrieve(gate, arrays, state, queries.shape[0])
    halves = [(a_own, swap(a_own, "c", 1)) for a_own in attended]

    def mm(side, k, adds, dtype):
        return project(at, halves[side], w_own, w_sib, k, adds, dtype)

    hops = ((1, 3), (3, 1))
    far = project_far(at, halves, w_own, w_far)
    far = [swap(far[i], "x", hops[i][0]) for i in range(2)]
    near = [mm(i, hops[i][0], (), BF16) for i in range(2)]
    far = [lax.optimization_barrier((far[i], near))[0] for i in range(2)]
    near = [swap(near[i], "x", hops[i][0]) for i in range(2)]
    passed = [swap(mm(i, hops[i][1], (far[i],), BF16), "x", hops[i][1]) for i in range(2)]
    mine = [mm(i, 0, (near[i],), F32) for i in range(2)]
    return finish(*mine, *passed)


def solution(mesh):
    finer = Mesh(mesh.devices.reshape(4, 8, 4, 2), ("y", "z", "x", "c"))
    rows, cols = ("y", "z"), ("x", "c")
    placed = (P(rows, cols), P(rows, cols), P(rows, cols), P(cols), P(cols, None))
    return jax.shard_map(
        local, mesh=finer, in_specs=placed, out_specs=P(rows, cols), check_vma=False
    )
```

```python
import functools
import math

import jax
import jax.numpy as jnp
from jax import lax
from jax.experimental import pallas as pl
from jax.experimental.pallas import tpu as pltpu
from jax.sharding import Mesh
from jax.sharding import PartitionSpec as P

HD = 128
REST = {0: 0, 1: 0, 3: 1}
PAD = 16
QB = 256
NT = (((1,), (1,)), ((), ()))
TN = (((0,), (0,)), ((), ()))
F32 = jnp.float32
BF16 = jnp.bfloat16
VMEM = pl.BlockSpec(memory_space=pltpu.VMEM)
SMEM = pl.BlockSpec(memory_space=pltpu.SMEM)
PARAMS = pltpu.CompilerParams(vmem_limit_bytes=8 * 2**20)


def near_core(array):
    return pltpu.with_memory_space_constraint(array, pltpu.VMEM)


def far_memory(array):
    return pltpu.with_memory_space_constraint(array, pltpu.HBM)


def features(v):
    return jnp.where(v > 0, v + 1.0, jnp.exp(jnp.minimum(v, 0.0)))


def delta_kernel(k_ref, v_ref, o_ref, total_ref, norm_ref):
    step = pl.program_id(0)
    heads = total_ref.shape[0] // HD

    @pl.when(step == 0)
    def _():
        total_ref[...] = jnp.zeros_like(total_ref)
        norm_ref[...] = jnp.zeros_like(norm_ref)

    feat = features(k_ref[...].astype(F32))
    norm_ref[...] += jnp.sum(feat, axis=0, keepdims=True)
    feat = feat.astype(BF16)
    for h in range(heads):
        cols = slice(h * HD, (h + 1) * HD)
        total_ref[cols, :] += lax.dot_general(
            v_ref[:, cols], feat[:, cols], TN, preferred_element_type=F32
        )

    @pl.when(step == pl.num_programs(0) - 1)
    def _():
        o_ref[: heads * HD, :] = total_ref[...].astype(BF16)
        row = lax.broadcasted_iota(jnp.int32, (PAD, HD), 0)
        norms = jnp.zeros((PAD, HD), F32)
        for h in range(heads):
            mine = jnp.broadcast_to(norm_ref[:, h * HD : (h + 1) * HD], (PAD, HD))
            norms = jnp.where(row == h, mine, norms)
        o_ref[heads * HD :, :] = norms.astype(BF16)


def delta(keys, values):
    rows, cols = keys.shape
    block = 512
    spec = pl.BlockSpec((block, cols), lambda i: (i, 0))
    return pl.pallas_call(
        delta_kernel,
        grid=(rows // block,),
        in_specs=[spec, spec],
        out_specs=VMEM,
        out_shape=pltpu.VMEM((cols + PAD, HD), BF16),
        scratch_shapes=[pltpu.VMEM((cols, HD), F32), pltpu.VMEM((1, cols), F32)],
        compiler_params=PARAMS,
        name="delta",
    )(far_memory(keys), far_memory(values))


def attention_kernel(first, g_ref, q_ref, k_ref, v_ref, o_ref, f_ref):
    h = pl.program_id(0)
    rows = q_ref.shape[0]
    c = math.log2(math.e) / math.sqrt(HD)
    keep = 1.0 - g_ref[first + h]
    causal = lax.broadcasted_iota(jnp.int32, (QB, QB), 1) <= lax.broadcasted_iota(
        jnp.int32, (QB, QB), 0
    )
    def scores(i):
        lo, hi = i * QB, (i + 1) * QB
        q = q_ref[lo:hi, :]
        diag = lax.dot_general(q, k_ref[lo:hi, :], NT, preferred_element_type=F32)
        diag = jnp.where(causal, diag, -1e30)
        if not lo:
            return diag, None
        return diag, lax.dot_general(q, k_ref[:lo, :], NT, preferred_element_type=F32)

    blocks = rows // QB
    ahead = scores(0)
    for i in range(blocks):
        lo, hi = i * QB, (i + 1) * QB
        diag, off = ahead
        if i + 1 < blocks:
            ahead = scores(i + 1)
        f_ref[0, lo:hi, :] = features(q_ref[lo:hi, :].astype(F32)).astype(BF16)
        top = jnp.max(diag, axis=-1, keepdims=True)
        if lo:
            top = jnp.maximum(top, jnp.max(off, axis=-1, keepdims=True))
        w = jnp.exp2((diag - top) * c)
        norm = jnp.sum(w, axis=-1, keepdims=True)
        out = jnp.dot(w.astype(BF16), v_ref[lo:hi, :], preferred_element_type=F32)
        if lo:
            w = jnp.exp2((off - top) * c)
            norm += jnp.sum(w, axis=-1, keepdims=True)
            out += jnp.dot(w.astype(BF16), v_ref[:lo, :], preferred_element_type=F32)
        o_ref[0, lo:hi, :] = out * (keep / norm)


def attention(gate, queries, keys, values, first, count):
    rows = queries.shape[0]
    spec = pl.BlockSpec((rows, HD), lambda h: (0, first + h))
    return pl.pallas_call(
        functools.partial(attention_kernel, first),
        grid=(count,),
        in_specs=[SMEM] + [spec] * 3,
        out_specs=[pl.BlockSpec((1, rows, HD), lambda h: (h, 0, 0))] * 2,
        out_shape=[pltpu.HBM((count, rows, HD), F32), pltpu.HBM((count, rows, HD), BF16)],
        compiler_params=PARAMS,
        name="attention",
    )(gate, far_memory(queries), far_memory(keys), far_memory(values))


def preload_kernel(*refs):
    half = len(refs) // 2
    sems = refs[-1]
    copies = [
        pltpu.make_async_copy(refs[i], refs[half + i], sems.at[i]) for i in range(half)
    ]
    for copy in copies:
        copy.start()
    for copy in copies:
        copy.wait()


def preload(arrays):
    return pl.pallas_call(
        preload_kernel,
        in_specs=[pl.BlockSpec(memory_space=pltpu.HBM)] * len(arrays),
        out_specs=[VMEM] * len(arrays),
        out_shape=[pltpu.VMEM(a.shape, a.dtype) for a in arrays],
        scratch_shapes=[pltpu.SemaphoreType.DMA((len(arrays),))],
        compiler_params=PARAMS,
        name="preload",
    )(*[far_memory(a) for a in arrays])


def retrieve_kernel(g_ref, *refs):
    *groups, s_ref, o1, o2 = refs
    rows = o1.shape[0]
    base = s_ref.shape[0] - PAD
    for side, o_ref in enumerate((o1, o2)):
        h = 0
        part = slice(side * rows, (side + 1) * rows)
        for group in range(0, len(groups), 2):
            local, feat = groups[group], groups[group + 1]
            for at in range(local.shape[0]):
                f = feat[at, part, :]
                numer = lax.dot_general(
                    f, s_ref[h * HD : (h + 1) * HD, :], NT, preferred_element_type=F32
                )
                denom = lax.dot_general(f, s_ref[base:, :], NT, preferred_element_type=F32)
                scale = g_ref[h] / jnp.maximum(denom[:, h : h + 1], 1.0)
                mixed = numer * scale + local[at, part, :]
                o_ref[:, h * HD : (h + 1) * HD] = mixed.astype(BF16)
                h += 1


def retrieve(gate, arrays, state, rows):
    cols = state.shape[0] - PAD
    return pl.pallas_call(
        retrieve_kernel,
        in_specs=[SMEM] + [VMEM] * (len(arrays) + 1),
        out_specs=[VMEM, VMEM],
        out_shape=[pltpu.VMEM((rows // 2, cols), BF16)] * 2,
        compiler_params=PARAMS,
        name="retrieve",
    )(gate, *[near_core(a) for a in arrays], near_core(state))


def sibling_kernel(at_ref, w_ref, far_ref, near_ref, mine_ref, sems):
    width = far_ref.shape[1]
    copies = []
    for k in range(4):
        to = lax.bitwise_xor(at_ref[0], k)
        cols = pl.ds(pl.multiple_of((2 * to + 1 - at_ref[1]) * width, width), width)
        target = far_ref if k == 2 else (near_ref if k else mine_ref).at[REST[k]]
        copies.append(pltpu.make_async_copy(w_ref.at[:, cols], target, sems.at[k]))
    for copy in copies:
        copy.start()
    for copy in copies:
        copy.wait()


def sibling_columns(at, weight):
    depth, cols = weight.shape
    return pl.pallas_call(
        sibling_kernel,
        in_specs=[SMEM, pl.BlockSpec(memory_space=pltpu.HBM)],
        out_specs=[VMEM] * 3,
        out_shape=[
            pltpu.VMEM((depth, cols // 8), BF16),
            pltpu.VMEM((2, depth, cols // 8), BF16),
            pltpu.VMEM((1, depth, cols // 8), BF16),
        ],
        scratch_shapes=[pltpu.SemaphoreType.DMA((4,))],
        compiler_params=PARAMS,
        name="sibling_columns",
    )(at, far_memory(weight))


def own_columns(at_ref, k, width):
    to = lax.bitwise_xor(at_ref[0], k)
    return pl.ds(pl.multiple_of((to * 2 + at_ref[1]) * width, width), width)


def far_own_kernel(at_ref, a1, a2, w_own, o1, o2):
    w = w_own[:, own_columns(at_ref, 2, o1.shape[1])]
    for a, o_ref in ((a1, o1), (a2, o2)):
        o_ref[...] = jnp.dot(a[...], w, preferred_element_type=F32)


def far_sibling_kernel(a1, a2, w_sib, p1, p2, o1, o2):
    w = w_sib[...]
    for a, p, o_ref in ((a1, p1, o1), (a2, p2, o2)):
        total = p[...] + jnp.dot(a[...], w, preferred_element_type=F32)
        o_ref[...] = total.astype(o_ref.dtype)


def project_far(at, halves, w_own, w_sib):
    rows, width = halves[0][0].shape[0], w_sib.shape[1]
    (own1, sib1), (own2, sib2) = halves
    partial = pl.pallas_call(
        far_own_kernel,
        in_specs=[SMEM] + [VMEM] * 3,
        out_specs=[VMEM, VMEM],
        out_shape=[pltpu.VMEM((rows, width), F32)] * 2,
        compiler_params=PARAMS,
        name="project_far_own",
    )(at, *[near_core(a) for a in (own1, own2, w_own)])
    return pl.pallas_call(
        far_sibling_kernel,
        in_specs=[VMEM] * 5,
        out_specs=[VMEM, VMEM],
        out_shape=[pltpu.VMEM((rows, width), BF16)] * 2,
        compiler_params=PARAMS,
        name="project_far",
    )(*[near_core(a) for a in (sib1, sib2, w_sib, *partial)])


def project_kernel(k, at_ref, a_own, a_sib, w_own, w_sib, *refs):
    *adds, o_ref = refs
    rows, width = o_ref.shape
    cols = own_columns(at_ref, k, width)
    block = 256
    for lo in range(0, rows, block):
        part = slice(lo, lo + block)
        total = jnp.dot(a_own[part, :], w_own[:, cols], preferred_element_type=F32)
        total += jnp.dot(a_sib[part, :], w_sib[REST[k]], preferred_element_type=F32)
        for add in adds:
            total += add[part, :].astype(F32)
        o_ref[part, :] = total.astype(o_ref.dtype)


def project(at, half, w_own, w_sib, k, adds, dtype):
    rows, width = half[0].shape[0], w_sib.shape[2]
    return pl.pallas_call(
        functools.partial(project_kernel, k),
        in_specs=[SMEM] + [VMEM] * (4 + len(adds)),
        out_specs=VMEM,
        out_shape=pltpu.VMEM((rows, width), dtype),
        compiler_params=PARAMS,
        name="project",
    )(at, *[near_core(a) for a in (*half, w_own, w_sib, *adds)])


def finish_kernel(p1, p2, r1, r2, o_ref, held, sems):
    rows = p1.shape[0]
    block = held.shape[0] // sems.shape[0]
    copies = []
    for i in range(sems.shape[0]):
        p, r = (p1, r1) if i * block < rows else (p2, r2)
        part = slice(i * block % rows, i * block % rows + block)
        out = slice(i * block, (i + 1) * block)
        held[out, :] = (p[part, :] + r[part, :].astype(F32)).astype(held.dtype)
        copies.append(pltpu.make_async_copy(held.at[out], o_ref.at[out], sems.at[i]))
        copies[-1].start()
    for copy in copies:
        copy.wait()


def finish(p1, p2, r1, r2):
    rows, width = p1.shape
    return pl.pallas_call(
        finish_kernel,
        in_specs=[VMEM] * 4,
        out_specs=pl.BlockSpec(memory_space=pltpu.HBM),
        out_shape=jax.ShapeDtypeStruct((2 * rows, width), BF16),
        scratch_shapes=[pltpu.VMEM((2 * rows, width), BF16), pltpu.SemaphoreType.DMA((4,))],
        compiler_params=PARAMS,
        name="finish",
    )(*[near_core(a) for a in (p1, p2, r1, r2)])


def swap(array, axis, mask):
    size = lax.axis_size(axis)
    return lax.ppermute(array, axis, [(i, i ^ mask) for i in range(size)])


def local(queries, keys, values, gate_bias, out_weight):
    y, z = lax.axis_index("y"), lax.axis_index("z")
    at = jnp.stack([lax.axis_index("x"), lax.axis_index("c")])
    heads = gate_bias.shape[0]
    gate = jax.nn.sigmoid(gate_bias)
    own = delta(keys, values)
    total, before = own.astype(F32), 0.0

    def fold(axis, mine, masks, beside):
        nonlocal total, before
        got = [swap(total.astype(BF16), axis, m) for m in masks]
        got, beside = lax.optimization_barrier((got, beside))
        for m, g in zip(masks, got):
            g = g.astype(F32)
            before = before + jnp.where((mine ^ m) < mine, g, 0.0)
            total = total + g
        total, before = lax.optimization_barrier((total, before))
        return beside

    weight, _ = lax.optimization_barrier((out_weight, own))
    w_out = fold("z", z, (1,), sibling_columns(at, weight))

    w_own, w_far = out_weight, swap(w_out[0], "c", 1)

    def heads_after(done):
        held, _ = lax.optimization_barrier(((queries, keys, values), done))
        return attention(gate, *held, 0, heads)

    waiting = fold("z", z, (5, 6, 2), heads_after(total))
    waiting, _ = lax.optimization_barrier((waiting, total))
    arrays, w_far = fold("y", y, (2, 1, 3), (preload(waiting), w_far))
    state = before.astype(BF16)
    w_rest, state = lax.optimization_barrier((w_out[1], state))
    w_sib = swap(w_rest, "c", 1)

    attended = retrieve(gate, arrays, state, queries.shape[0])
    halves = [(a_own, swap(a_own, "c", 1)) for a_own in attended]

    def mm(side, k, adds, dtype):
        return project(at, halves[side], w_own, w_sib if k else w_mine, k, adds, dtype)

    hops = ((1, 3), (3, 1))
    far = project_far(at, halves, w_own, w_far)
    far = [swap(far[i], "x", hops[i][0]) for i in range(2)]
    near = [mm(i, hops[i][0], (), BF16) for i in range(2)]
    far = [lax.optimization_barrier((far[i], near))[0] for i in range(2)]
    w_mine, _ = lax.optimization_barrier((w_out[2], near))
    w_mine = swap(w_mine, "c", 1)
    near = [swap(near[i], "x", hops[i][0]) for i in range(2)]
    passed = [swap(mm(i, hops[i][1], (far[i],), BF16), "x", hops[i][1]) for i in range(2)]
    mine = [mm(i, 0, (near[i],), F32) for i in range(2)]
    return finish(*mine, *passed)


def solution(mesh):
    finer = Mesh(mesh.devices.reshape(4, 8, 4, 2), ("y", "z", "x", "c"))
    rows, cols = ("y", "z"), ("x", "c")
    placed = (P(rows, cols), P(rows, cols), P(rows, cols), P(cols), P(cols, None))
    return jax.shard_map(
        local, mesh=finer, in_specs=placed, out_specs=P(rows, cols), check_vma=False
    )
```
